32 devices in a mesh: dp: 8 (over z, y), ctx: 4 (over x, core).
Axes of the slice: x: 2, y: 2, z: 4, core: 2. Of those that a mesh axis runs over, the one named last changes fastest.
Arguments:
- queries: bfloat16 [8, 512, 4096], P('dp', 'ctx'), may hold values from -9 to 9
- keys: bfloat16 [8, 512, 512], P('dp', 'ctx'), may hold values from -7 to 7
- values: bfloat16 [8, 512, 512], P('dp', 'ctx'), may hold values from -6 to 6
- cotangent: bfloat16 [8, 512, 4096], P('dp', 'ctx'), may hold values from -6 to 6
- live: int32 [8, 512], P('dp', 'ctx'), may hold values from 0 to 1, as said below
- docs: int32 [8, 512], P('dp'), may hold values from 0 to 5, never falling along the last dimension, each value on 1 to 256 neighbouring positions
Outputs:
- attended: bfloat16 [8, 512, 4096], P('dp', 'ctx')
- grad_queries: bfloat16 [8, 512, 4096], P('dp', 'ctx')
- key_gradient: bfloat16 [8, 512, 512], P('dp', 'ctx')
- value_gradient: bfloat16 [8, 512, 512], P('dp', 'ctx')
The draws below stay inside these ranges and needn't reach their ends.
Inputs may be any that keep to these rules, and one draw needn't show every extreme that they name: `docs`: never falls along a sequence; each document spans 1 to 256 positions and one spans exactly 256. `live`: row 0 of every sequence is 1.
All inputs are finite; a program needn't handle non-finite values.
Results may differ from the reference program's by a relative error of at most 0.02.
Values may be sent and summed in bfloat16 or wider, within the bound.
A program may use at most 64 MiB of HBM per device.

```python
import math
import jax
import jax.numpy as jnp
import numpy as np
from jax import lax

QUERY_HEADS = 32
KEY_VALUE_HEADS = 4
HEAD_SIZE = 128
TOK_DEV = 128
DOCS = 6
SEQUENCE_TOKENS = 512
BATCH_SEQUENCES = 8
N_CTX = 4


def draw_queries(key, part):
    query_group_width = QUERY_HEADS // KEY_VALUE_HEADS
    array_shape = (BATCH_SEQUENCES, SEQUENCE_TOKENS, KEY_VALUE_HEADS, query_group_width, HEAD_SIZE)
    final_result = jnp.clip(jax.random.normal(jax.random.fold_in(key, 1), array_shape, jnp.float32), -6.0, 6.0)
    return final_result.reshape(BATCH_SEQUENCES, SEQUENCE_TOKENS, QUERY_HEADS * HEAD_SIZE).astype(jnp.bfloat16)


def draw_keys(key, part):
    array_shape = (BATCH_SEQUENCES, SEQUENCE_TOKENS, KEY_VALUE_HEADS, HEAD_SIZE)
    final_result = jnp.clip(jax.random.normal(jax.random.fold_in(key, 11), array_shape, jnp.float32), -6.0, 6.0)
    return final_result.reshape(BATCH_SEQUENCES, SEQUENCE_TOKENS, KEY_VALUE_HEADS * HEAD_SIZE).astype(jnp.bfloat16)


def draw_live(key, part):
    sequence_ids = jnp.arange(BATCH_SEQUENCES, dtype=jnp.int32)[:, None]
    cutoff = 250 + 500 * sequence_ids // max(BATCH_SEQUENCES - 1, 1)
    picks = jax.random.randint(key, (BATCH_SEQUENCES, SEQUENCE_TOKENS), 0, 1000, dtype=jnp.int32)
    counted = (picks < cutoff).astype(jnp.int32)
    first_row = jnp.arange(SEQUENCE_TOKENS, dtype=jnp.int32)[None, :] == 0
    return jnp.where(first_row, 1, counted).astype(jnp.int32)


def level_of(own_key, shape, cuts, smallest, top_value):
    level, own = 1.0, jax.random.fold_in(own_key, 6)
    for axis_at, shards_of in cuts:
        draws = jnp.exp(jax.random.uniform(jax.random.fold_in(own, axis_at), (shards_of,), jnp.float32, smallest / len(cuts), top_value / len(cuts)))
        level = level * jnp.repeat(draws, shape[axis_at] // shards_of).reshape([-1 if axis == axis_at else 1 for axis in range(len(shape))])
    return level


def profile(number_of, total, bound, lean):
    loads = [(1 << 20) // math.isqrt(grade ** lean) + 1 for grade in range(2, number_of + 1)]
    rest, given = total - bound - (number_of - 1), [1] * (number_of - 1)
    while rest > 0:
        free = [i for i in range(number_of - 1) if given[i] < bound]
        whole, remaining = sum([loads[i] for i in free]), rest
        for i in free:
            more = min(bound - given[i], max(1, remaining * loads[i] // whole), rest)
            given[i] = given[i] + more
            rest = rest - more
    return np.array([bound] + given)


def uneven_parts(own_key, count, total, limit, slope):
    if count == 2:
        one = jax.random.randint(own_key, (), max(1, total - limit), min(limit, total - 1) + 1)
        return jnp.stack([one, total - one])
    lengths = jnp.asarray(profile(count, total, limit, slope), jnp.int32)
    twos = (count - 1) // 2
    giver, taker = lengths[1:1 + 2 * twos:2], lengths[2:2 + 2 * twos:2]
    margin = jnp.minimum(giver - 1, limit - taker)
    moved = jax.random.randint(jax.random.fold_in(own_key, 1), (twos,), 0, 1 << 20) % (margin + 1)
    lengths = lengths.at[1:1 + 2 * twos:2].set(giver - moved).at[2:2 + 2 * twos:2].set(taker + moved)
    return lengths[jax.random.permutation(jax.random.fold_in(own_key, 2), count)]


def gaussian(stream_key, shape, scale, bound, pieces=(), held_as=jnp.bfloat16):
    array = scale * jax.random.normal(stream_key, shape, jnp.float32)
    if pieces:
        array = array * level_of(stream_key, shape, pieces, -0.22, 0.18)
    return jnp.clip(array, -bound, bound).astype(held_as)


def setup_inputs(seed: int = 0) -> dict:
    arg_keys = jax.random.split(jax.random.key(seed), 7)
    return {
        "queries": draw_queries(jax.random.fold_in(arg_keys[6], 71), 0),
        "keys": draw_keys(jax.random.fold_in(arg_keys[6], 71), 0),
        "values": gaussian(arg_keys[2], (BATCH_SEQUENCES, SEQUENCE_TOKENS, KEY_VALUE_HEADS * HEAD_SIZE), 1.0, 6.0, ((0, 8), (1, 4))),
        "cotangent": gaussian(arg_keys[3], (BATCH_SEQUENCES, SEQUENCE_TOKENS, QUERY_HEADS * HEAD_SIZE), 1.0, 6.0, ((0, 8), (1, 4))),
        "live": draw_live(jax.random.fold_in(arg_keys[6], 71), 0),
        "docs": jax.vmap(lambda own: jnp.searchsorted(jnp.cumsum(uneven_parts(own, DOCS, SEQUENCE_TOKENS, SEQUENCE_TOKENS // 2, 1)), jnp.arange(SEQUENCE_TOKENS), side="right"))(jax.random.split(arg_keys[5], BATCH_SEQUENCES)).reshape((BATCH_SEQUENCES, SEQUENCE_TOKENS)).astype(jnp.int32),
    }


masked_fill = -1e+30

def folded_positions():
    half_rows = TOK_DEV // 2
    offsets = jnp.arange(SEQUENCE_TOKENS, dtype=jnp.int32)
    slot_index = offsets // half_rows
    device = slot_index // 2
    piece_id = jnp.where(slot_index % 2 == 0, device, 2 * N_CTX - 1 - device)
    return piece_id * half_rows + offsets % half_rows

def one_head(query_head, grad_head, key_natural, value_natural, docs):
    score_scale = 1.0 / math.sqrt(HEAD_SIZE)
    half_rows = TOK_DEV // 2
    outs_list, rows_list = ([], [])
    key_total = jnp.zeros((SEQUENCE_TOKENS, HEAD_SIZE), query_head.dtype)
    value_total = jnp.zeros((SEQUENCE_TOKENS, HEAD_SIZE), query_head.dtype)
    for block in range(N_CTX):
        key_block = jnp.zeros((SEQUENCE_TOKENS, HEAD_SIZE), query_head.dtype)
        value_block = jnp.zeros((SEQUENCE_TOKENS, HEAD_SIZE), query_head.dtype)
        for side in range(2):
            piece_id = block if side == 0 else 2 * N_CTX - 1 - block
            row_start = block * TOK_DEV + side * half_rows
            span = (piece_id + 1) * half_rows
            query_part = query_head[row_start:row_start + half_rows]
            grad_part = grad_head[row_start:row_start + half_rows]
            key_part = key_natural[:span]
            value_part = value_natural[:span]
            query_pos = piece_id * half_rows + jnp.arange(half_rows, dtype=jnp.int32)
            key_pos = jnp.arange(span, dtype=jnp.int32)
            query_doc = docs[piece_id * half_rows:(piece_id + 1) * half_rows]
            allowed = (query_doc[:, None] == docs[:span][None, :]) & (key_pos[None, :] <= query_pos[:, None])
            scores = jnp.einsum('qjd,kd->jqk', query_part, key_part) * score_scale
            masked = jnp.where(allowed, scores, masked_fill)
            row_peak = lax.optimization_barrier(jnp.max(masked, axis=-1, keepdims=True))
            log_total = row_peak + jnp.log(lax.optimization_barrier(jnp.sum(jnp.exp(masked - row_peak), axis=-1, keepdims=True)))
            weights = jnp.where(allowed, jnp.exp(masked - log_total), 0.0)
            rounded = weights.astype(jnp.bfloat16).astype(query_head.dtype)
            attended = jnp.einsum('jqk,kd->qjd', rounded, value_part).astype(jnp.bfloat16)
            delta = jnp.transpose(lax.optimization_barrier(jnp.sum(grad_part * attended.astype(query_head.dtype), axis=-1)))[:, :, None]
            pushes = jnp.einsum('qjd,kd->jqk', grad_part, value_part)
            slopes = (weights * (pushes - delta) * score_scale).astype(jnp.bfloat16).astype(query_head.dtype)
            grad_rows = jnp.einsum('jqk,kd->qjd', slopes, key_part).astype(jnp.bfloat16)
            key_term = jnp.einsum('jqk,qjd->kd', slopes, query_part)
            value_term = jnp.einsum('jqk,qjd->kd', rounded, grad_part)
            key_block = key_block.at[:span].add(key_term)
            value_block = value_block.at[:span].add(value_term)
            outs_list.append(attended)
            rows_list.append(grad_rows)
        key_total = key_total + lax.optimization_barrier(key_block.astype(jnp.bfloat16)).astype(query_head.dtype)
        value_total = value_total + lax.optimization_barrier(value_block.astype(jnp.bfloat16)).astype(query_head.dtype)
    return (jnp.concatenate(outs_list, axis=0), jnp.concatenate(rows_list, axis=0), key_total.astype(jnp.bfloat16), value_total.astype(jnp.bfloat16))

def one_sequence(queries, keys, values, cotangent, live, docs, loss_ratio):
    query_group_width = QUERY_HEADS // KEY_VALUE_HEADS
    positions = folded_positions()
    inverse = jnp.zeros((SEQUENCE_TOKENS,), jnp.int32).at[positions].set(jnp.arange(SEQUENCE_TOKENS, dtype=jnp.int32))
    work_type = loss_ratio.dtype
    output_gradient = (cotangent.astype(work_type) * live.astype(work_type)[:, None] * loss_ratio).astype(jnp.bfloat16)
    query_heads = jnp.transpose(queries.reshape(SEQUENCE_TOKENS, KEY_VALUE_HEADS, query_group_width, HEAD_SIZE).astype(work_type), (1, 0, 2, 3))
    grad_heads = jnp.transpose(output_gradient.reshape(SEQUENCE_TOKENS, KEY_VALUE_HEADS, query_group_width, HEAD_SIZE).astype(work_type), (1, 0, 2, 3))
    key_heads = jnp.transpose(jnp.take(keys, inverse, axis=0).reshape(SEQUENCE_TOKENS, KEY_VALUE_HEADS, HEAD_SIZE).astype(work_type), (1, 0, 2))
    value_heads = jnp.transpose(jnp.take(values, inverse, axis=0).reshape(SEQUENCE_TOKENS, KEY_VALUE_HEADS, HEAD_SIZE).astype(work_type), (1, 0, 2))

    def per_head(operands):
        return one_head(operands[0], operands[1], operands[2], operands[3], docs)
    attended, grad_rows, key_sum, value_sum = lax.map(per_head, (query_heads, grad_heads, key_heads, value_heads))
    attended_all = jnp.transpose(attended, (1, 0, 2, 3)).reshape(SEQUENCE_TOKENS, QUERY_HEADS * HEAD_SIZE)
    grad_queries = jnp.transpose(grad_rows, (1, 0, 2, 3)).reshape(SEQUENCE_TOKENS, QUERY_HEADS * HEAD_SIZE)
    key_gradient = jnp.take(jnp.transpose(key_sum, (1, 0, 2)), positions, axis=0).reshape(SEQUENCE_TOKENS, KEY_VALUE_HEADS * HEAD_SIZE)
    value_gradient = jnp.take(jnp.transpose(value_sum, (1, 0, 2)), positions, axis=0).reshape(SEQUENCE_TOKENS, KEY_VALUE_HEADS * HEAD_SIZE)
    return (attended_all, grad_queries, key_gradient, value_gradient)

def reference(queries, keys, values, cotangent, live, docs):
    live_count = jnp.sum(live).astype(jnp.float32)
    loss_ratio = float(BATCH_SEQUENCES * SEQUENCE_TOKENS) / live_count

    def per_sequence(operands):
        return one_sequence(operands[0], operands[1], operands[2], operands[3], operands[4], operands[5], loss_ratio)
    return lax.map(per_sequence, (queries, keys, values, cotangent, live, docs))
```

```python
import functools
import math

import jax
import jax.numpy as jnp
from jax import lax
from jax.experimental import pallas as pl
from jax.experimental.pallas import tpu as pltpu
from jax.sharding import PartitionSpec as P

HEAD_SIZE = 128
MESH = pl.DeviceIdType.MESH
masked_fill = -1e30
f32, bf16 = jnp.float32, jnp.bfloat16


def matmul(a, b):
    return jnp.dot(a, b, preferred_element_type=f32)


def matmul_nt(a, b):
    return lax.dot_general(a, b, (((1,), (1,)), ((), ())), preferred_element_type=f32)


def on(condition, action):
    pl.when(condition)(action)


def one(condition):
    return jnp.where(condition, 1, 0)


def kernel(
    n, depth, q_hbm, k_hbm, v_hbm, c_hbm, live_hbm, docs_hbm,
    att, gq, kg_ref, vg_ref, total_ref,
    q, cot, kv, tx, px, rx, acc_k, acc_v, held_p, held_s, bias_a, bias_b,
    docs_ref, doc_col, live_row, live_rows, live_all, live_sum, live_pair,
    in_sem, far_sent, far_got, pass_sent, own_got, pass_got,
    part_sent, part_got, part_own, back_sent, back_got, live_sem,
):
    rows = q.shape[0]
    half_rows = rows // 2
    groups = kv.shape[0]
    width = q.shape[1] // groups
    heads = width // HEAD_SIZE
    lanes = heads * half_rows
    chunks = 2 * n
    chips = n // 2
    few = 2
    me, my_dp = lax.axis_index("ctx"), lax.axis_index("dp")
    chip, core = me // 2, lax.rem(me, 2)
    partner = me + 1 - 2 * core
    near = chip == 0
    root = my_dp == 0
    exp_scale = math.log2(math.e) / math.sqrt(HEAD_SIZE)

    def chunk_of(device, half):
        return device if half == 0 else chunks - 1 - device

    def needs(device, chunk):
        first = chunk <= device
        second = (chunk >= n - 1 - device) & (chunk <= chunks - 1 - device)
        return first | second

    def chip_needs(a_chip, chunk):
        return needs(2 * a_chip, chunk) | needs(2 * a_chip + 1, chunk)

    def chip_ahead(k):
        return lax.rem(chip + k, chips)

    def chip_behind(k):
        return lax.rem(chip + chips - k, chips)

    def cross(a_chip):
        return 2 * a_chip + 1 - core

    def level(a_chip):
        return 2 * a_chip + core

    def across(k):
        return cross(chip_ahead(k))

    barrier = pltpu.get_barrier_semaphore()

    def greet(dp, ctx):
        pl.semaphore_signal(barrier, inc=1, device_id=(dp, ctx), device_id_type=MESH)

    greet(my_dp, partner)
    for k in range(1, chips):
        greet(my_dp, across(k))

    def own_copy(g, half, which):
        source = k_hbm if which == 0 else v_hbm
        return pltpu.make_async_copy(
            source.at[pl.ds(half * half_rows, half_rows), pl.ds(g * HEAD_SIZE, HEAD_SIZE)],
            kv.at[g, chunk_of(me, half), which],
            in_sem.at[0],
        )

    for g in range(groups):
        for half in range(2):
            for which in range(2):
                own_copy(g, half, which).start()
    live_copy = pltpu.make_async_copy(live_hbm, live_row, in_sem.at[1])
    docs_copy = pltpu.make_async_copy(docs_hbm, docs_ref, in_sem.at[2])
    q_copy = pltpu.make_async_copy(q_hbm, q, in_sem.at[3])
    c_copy = pltpu.make_async_copy(c_hbm, cot, in_sem.at[4])
    live_copy.start()
    docs_copy.start()
    c_copy.start()
    q_copy.start()

    @pl.when(root)
    def _():
        def greet_dp(d, carry):
            greet(d, me)
            for k in range(1, chips):
                greet(d, across(k))
            return carry

        lax.fori_loop(1, depth, greet_dp, 0)

    def chunk_copy(source, target, sent, got, device):
        return pltpu.make_async_remote_copy(
            src_ref=source, dst_ref=target, send_sem=sent, recv_sem=got,
            device_id=device, device_id_type=MESH,
        )

    def far_copy(g, k, chunk):
        return chunk_copy(
            kv.at[g, chunk], kv.at[g, chunk], far_sent, far_got.at[g, k - 1],
            (my_dp, across(k)),
        )

    def pass_copy(g, k, chunk):
        got = own_got if k == 0 else pass_got.at[g, k - 1]
        return chunk_copy(kv.at[g, chunk], kv.at[g, chunk], pass_sent, got, (my_dp, partner))

    def part_copy(g, k, chunk):
        got = part_own if k == 0 else part_got.at[g, k - 1]
        return chunk_copy(tx.at[g, chunk], px.at[g, chunk], part_sent, got, (my_dp, partner))

    def back_copy(g, k, half, chunk):
        return chunk_copy(
            tx.at[g, chunk], rx.at[g, k - 1, half], back_sent, back_got,
            (my_dp, across(k)),
        )

    def wait_chunks(sem, count, most, whole):
        for c in range(1, most + 1):
            block = kv.at[:, 0:c] if whole else kv.at[0, 0:c]
            on(count == c, lambda: pltpu.make_async_copy(block, block, sem).wait())

    def pair(condition):
        return one(condition(0)) + one(condition(1))

    def over_chips(condition):
        count = 0
        for k in range(1, chips):
            count += pair(lambda half: condition(k, half))
        return count

    def sends_far(k, half):
        return chip_needs(chip_ahead(k), chunk_of(me, half))

    def gets_far(k, half):
        return chip_needs(chip, chunk_of(cross(chip_behind(k)), half))

    def passes(k, half):
        return needs(partner, chunk_of(cross(chip_behind(k)), half))

    def gets_passed(k, half):
        return needs(me, chunk_of(level(chip_behind(k)), half))

    def parts_out(k, half):
        return needs(me, chunk_of(level(chip_ahead(k)), half))

    def gets_part(k, half):
        return needs(partner, chunk_of(cross(chip_ahead(k)), half))

    def sends_back(k, half):
        return chip_needs(chip, chunk_of(cross(chip_ahead(k)), half))

    def gets_back(k, half):
        return chip_needs(chip_behind(k), chunk_of(me, half))

    def shares(half):
        return needs(partner, chunk_of(me, half))

    def shared(half):
        return needs(me, chunk_of(partner, half))

    def arrive(g):
        for k in range(1, chips):
            wait_chunks(far_got.at[g, k - 1], pair(lambda half: gets_far(k, half)), 2, False)
            for half in range(2):
                chunk = chunk_of(cross(chip_behind(k)), half)
                on(passes(k, half), lambda: pass_copy(g, k, chunk).start())

    def settle(g):
        for k in range(1, chips):
            wait_chunks(pass_got.at[g, k - 1], pair(lambda half: gets_passed(k, half)), 2, False)

    def send_parts(g):
        for k in range(1, chips):
            for half in range(2):
                chunk = chunk_of(level(chip_ahead(k)), half)
                on(parts_out(k, half), lambda: part_copy(g, k, chunk).start())
        for half in range(2):
            chunk = chunk_of(partner, half)
            on(shared(half), lambda: part_copy(g, 0, chunk).start())

    def combine(g):
        for k in range(1, chips):
            wait_chunks(part_got.at[g, k - 1], pair(lambda half: gets_part(k, half)), 2, False)
            for half in range(2):
                chunk = chunk_of(cross(chip_ahead(k)), half)

                @pl.when(gets_part(k, half))
                def _(chunk=chunk):
                    tx[g, chunk] = (tx[g, chunk].astype(f32) + px[g, chunk].astype(f32)).astype(
                        bf16
                    )

                on(sends_back(k, half), lambda: back_copy(g, k, half, chunk).start())

    def live_copy_to(k):
        device = me if k == 0 else across(k)
        return chunk_copy(
            live_row, live_all.at[my_dp * chips + k], live_sem.at[0], live_sem.at[1], (0, device)
        )

    def pair_copy():
        return chunk_copy(
            live_sum, live_pair, live_sem.at[2], live_sem.at[3], (my_dp, partner)
        )

    def total_copy(d):
        return chunk_copy(total_ref, total_ref, live_sem.at[4], live_sem.at[5], (d, me))

    def wait_rows(sem, count):
        block = live_all.at[0:count]
        pltpu.make_async_copy(block, block, sem).wait()

    def gather_live():
        wait_rows(live_sem.at[1], depth * chips - 1)
        live_sum[...] = live_row[...] + jnp.sum(live_all[1:], axis=0)
        pair_copy().start()

    def spread_live():
        pair_copy().wait_recv()
        total_ref[...] = live_sum[...] + live_pair[...]

        def spread(d, carry):
            total_copy(d).start()
            return carry

        lax.fori_loop(1, depth, spread, 0)

    own = kv.at[:, 0:2]
    live_copy.wait()
    pltpu.make_async_copy(own, own, in_sem.at[0]).wait()
    pl.semaphore_wait(barrier, chips + jnp.where(root, 0, chips))
    for k in range(1, chips):
        live_copy_to(k).start()

    def send_keys(g, carry):
        for k in range(1, chips):
            for half in range(2):
                chunk = chunk_of(me, half)
                on(sends_far(k, half), lambda: far_copy(g, k, chunk).start())
        return carry

    lax.fori_loop(0, groups, send_keys, 0)

    def share_keys(g, carry):
        for half in range(2):
            chunk = chunk_of(me, half)
            on(shares(half), lambda: pass_copy(g, 0, chunk).start())
        return carry

    lax.fori_loop(0, groups, share_keys, 0)
    on(jnp.logical_not(root), lambda: live_copy_to(0).start())

    def clear(chunk, carry):
        enters = (lax.rem(chunk, 2) != core) & (chunk // 2 != chip)
        held = needs(me, chunk) | (enters & chip_needs(chip, chunk))

        @pl.when(jnp.logical_not(held))
        def _():
            for g in range(groups):
                kv[g, chunk] = jnp.zeros(kv.shape[2:], bf16)

        return carry

    lax.fori_loop(0, n, clear, 0)
    tx[...] = jnp.zeros(tx.shape, bf16)
    acc_k[...] = jnp.zeros(acc_k.shape, f32)
    acc_v[...] = jnp.zeros(acc_v.shape, f32)

    docs_copy.wait()
    for b in range(doc_col.shape[0] // HEAD_SIZE):
        piece = docs_ref[0:1, b * HEAD_SIZE:(b + 1) * HEAD_SIZE].astype(f32)
        doc_col[b * HEAD_SIZE:(b + 1) * HEAD_SIZE, :] = jnp.transpose(
            jnp.broadcast_to(piece, (HEAD_SIZE, HEAD_SIZE))
        )
    first_b = n - 1 - me

    def build(bias, key_chunk, query_chunk):
        size = bias.shape[0]
        start = key_chunk * half_rows
        key_doc = doc_col[pl.ds(pl.multiple_of(start, half_rows), size), 0:1]
        key_pos = start + lax.broadcasted_iota(jnp.int32, (size, rows), 0)
        query_pos = query_chunk * half_rows + lax.rem(
            lax.broadcasted_iota(jnp.int32, (size, rows), 1), half_rows
        )
        query_doc = jnp.sum(
            jnp.where(key_pos == query_pos, key_doc, 0.0), axis=0, keepdims=True
        )
        allowed = (key_doc == query_doc) & (key_pos <= query_pos)
        bias[...] = jnp.where(allowed, 0.0, masked_fill)

    build(bias_a, 0, chunk_of(me, 0))
    build(bias_b, first_b, chunk_of(me, 1))
    live_rows[...] = jnp.transpose(
        jnp.broadcast_to(live_row[...].astype(f32), (HEAD_SIZE, rows))
    )
    c_copy.wait()

    def keep_live(j, carry):
        columns = pl.ds(pl.multiple_of(j * HEAD_SIZE, HEAD_SIZE), HEAD_SIZE)
        cot[:, columns] = (cot[:, columns].astype(f32) * live_rows[...]).astype(bf16)
        return carry

    lax.fori_loop(0, groups * heads, keep_live, 0, unroll=4)
    q_copy.wait()
    wait_chunks(own_got, pair(shared), 2, True)

    def stacked(source, g, half):
        return jnp.concatenate(
            [
                source[
                    half * half_rows:(half + 1) * half_rows,
                    pl.ds(pl.multiple_of(g * width + j * HEAD_SIZE, HEAD_SIZE), HEAD_SIZE),
                ]
                for j in range(heads)
            ],
            axis=0,
        )

    def attend(g, half, start, count, add):
        size = count * half_rows
        window = pl.ds(start, count)
        keys = kv[g, window, 0].reshape(size, HEAD_SIZE)
        values = kv[g, window, 1].reshape(size, HEAD_SIZE)
        queries = stacked(q, g, half)
        grads = stacked(cot, g, half)
        bias = (bias_a if half == 0 else bias_b)[0:size]
        bias = jnp.concatenate([bias] * (lanes // rows), axis=1)
        scores = matmul_nt(keys, queries) + bias
        pushes = matmul_nt(values, grads)
        peak = jnp.max(scores, axis=0, keepdims=True)
        mass = jnp.exp2((scores - peak) * exp_scale)
        total = jnp.sum(mass, axis=0, keepdims=True)
        weights = mass * (1.0 / total)
        rounded = weights.astype(bf16)
        pushed = weights * pushes
        delta = jnp.sum(pushed, axis=0, keepdims=True)
        slopes = (pushed - weights * delta).astype(bf16)
        held_p[half, 0:size] = rounded
        held_s[half, 0:size] = slopes
        value_part = matmul(rounded, grads).reshape(count, half_rows, HEAD_SIZE)
        key_part = matmul(slopes, queries).reshape(count, half_rows, HEAD_SIZE)
        if half == 0 and add:
            acc_k[0:count] = key_part
            acc_v[0:count] = value_part
        elif add:
            key_part += acc_k[window]
            value_part += acc_v[window]
        tx[g, window, 0] = key_part.astype(bf16)
        tx[g, window, 1] = value_part.astype(bf16)

    def finish(g, half, start, count):
        size = count * half_rows
        window = pl.ds(start, count)
        low, high = half * half_rows, (half + 1) * half_rows
        keys = kv[g, window, 0].reshape(size, HEAD_SIZE)
        values = kv[g, window, 1].reshape(size, HEAD_SIZE)
        out = jnp.transpose(matmul(jnp.transpose(values), held_p[half, 0:size]).astype(bf16))
        grad_rows = jnp.transpose(matmul(jnp.transpose(keys), held_s[half, 0:size]).astype(bf16))
        for j in range(heads):
            wide = pl.ds(pl.multiple_of(g * width + j * HEAD_SIZE, HEAD_SIZE), HEAD_SIZE)
            att[low:high, wide] = out[j * half_rows:(j + 1) * half_rows, :]
            gq[low:high, wide] = grad_rows[j * half_rows:(j + 1) * half_rows, :]

    def near_first(g, carry):
        attend(g, 0, 0, few, False)
        finish(g, 0, 0, few)
        return carry

    def near_step(g, carry):
        arrive(g)
        on(g > 0, lambda: finish(g - 1, 1, first_b, n + 1))
        on(g > 0, lambda: combine(g - 1))
        settle(g)
        attend(g, 1, first_b, n + 1, False)
        send_parts(g)
        on(root & (g == groups - 2), gather_live)
        return carry

    def far_step(g, carry):
        settle(g)
        attend(g, 0, 0, n, True)
        on(g + 1 < groups, lambda: arrive(g + 1))
        on(g > 0, lambda: combine(g - 1))
        attend(g, 1, first_b, n + 1, True)
        send_parts(g)
        finish(g, 0, 0, n)

        @pl.when(g + 1 < groups)
        def _():
            finish(g, 1, first_b, n + 1)

        on(root & (g == groups - 2), gather_live)
        return carry

    @pl.when(near)
    def _():
        lax.fori_loop(0, groups, near_first, 0)
        lax.fori_loop(0, groups, near_step, 0)

    @pl.when(jnp.logical_not(near))
    def _():
        arrive(0)
        lax.fori_loop(0, groups, far_step, 0)

    on(root, spread_live)
    combine(groups - 1)
    finish(groups - 1, 1, first_b, n + 1)
    on(jnp.logical_not(root), lambda: total_copy(0).wait_recv())
    wait_chunks(part_own, pair(shares), 2, True)
    wait_chunks(back_got, over_chips(gets_back), chunks - 2, True)

    def reduce_step(g, carry):
        columns = pl.ds(pl.multiple_of(g * HEAD_SIZE, HEAD_SIZE), HEAD_SIZE)
        for half in range(2):
            mine = chunk_of(me, half)
            low, high = half * half_rows, (half + 1) * half_rows
            kg_ref[low:high, columns] = tx[g, mine, 0].astype(f32)
            vg_ref[low:high, columns] = tx[g, mine, 1].astype(f32)

            @pl.when(shares(half))
            def _(mine=mine, low=low, high=high):
                kg_ref[low:high, columns] += px[g, mine, 0].astype(f32)
                vg_ref[low:high, columns] += px[g, mine, 1].astype(f32)

            for k in range(1, chips):

                @pl.when(gets_back(k, half))
                def _(k=k, half=half, low=low, high=high):
                    kg_ref[low:high, columns] += rx[g, k - 1, half, 0].astype(f32)
                    vg_ref[low:high, columns] += rx[g, k - 1, half, 1].astype(f32)

        return carry

    lax.fori_loop(0, groups, reduce_step, 0)

    wait_chunks(far_sent, over_chips(sends_far), chunks - 2, True)
    wait_chunks(pass_sent, over_chips(passes) + pair(shares), chunks, True)
    wait_chunks(part_sent, over_chips(parts_out) + pair(shared), chunks, True)
    wait_chunks(back_sent, over_chips(sends_back), chunks - 2, True)

    @pl.when(root)
    def _():
        wait_rows(live_sem.at[0], chips - 1)
        pair_copy().wait_send()
        wait_rows(live_sem.at[4], depth - 1)

    on(jnp.logical_not(root), lambda: wait_rows(live_sem.at[0], chips))


def store_kernel(
    scale, att, gq32, kg32, vg32, total_ref, att_out, gq_out, kg_out, vg_out, gq, kg, vg, sem
):
    copies = []

    def put(source, target):
        copies.append(pltpu.make_async_copy(source, target, sem.at[len(copies)]))
        copies[-1].start()

    put(att, att_out)
    ratio = scale / jnp.sum(total_ref[...].astype(f32), axis=1, keepdims=True)
    slope_ratio = ratio * (1.0 / math.sqrt(HEAD_SIZE))
    pieces = sem.shape[0] - 3
    width = gq.shape[1] // pieces
    for g in range(pieces):
        wide = pl.ds(g * width, width)
        gq[:, wide] = (gq32[:, wide].astype(f32) * slope_ratio).astype(bf16)
        put(gq.at[:, wide], gq_out.at[:, wide])
    kg[...] = (kg32[...] * slope_ratio).astype(bf16)
    put(kg, kg_out)
    vg[...] = (vg32[...] * ratio).astype(bf16)
    put(vg, vg_out)
    for copy in copies:
        copy.wait()


def on_device(n, depth, queries, keys, values, cotangent, live, docs):
    rows, q_width = queries.shape[1:]
    kv_width = keys.shape[2]
    groups = kv_width // HEAD_SIZE
    width = q_width // groups
    half_rows = rows // 2
    lanes = width // HEAD_SIZE * half_rows
    chunks = 2 * n
    chips = n // 2
    if n % 2 or n < 4 or depth < 2:
        raise ValueError("mesh")
    anywhere = pl.BlockSpec(memory_space=pl.ANY)
    vmem = pl.BlockSpec(memory_space=pltpu.VMEM)
    dma = pltpu.SemaphoreType.DMA
    block = (2, half_rows, HEAD_SIZE)
    most = (n + 1) * half_rows
    results = pl.pallas_call(
        functools.partial(kernel, n, depth),
        out_shape=(
            pltpu.VMEM((rows, q_width), bf16),
            pltpu.VMEM((rows, q_width), bf16),
            pltpu.VMEM((rows, kv_width), f32),
            pltpu.VMEM((rows, kv_width), f32),
            pltpu.VMEM((1, rows), jnp.int32),
        ),
        in_specs=[anywhere] * 6,
        out_specs=(vmem,) * 5,
        scratch_shapes=[
            pltpu.VMEM((rows, q_width), bf16),
            pltpu.VMEM((rows, q_width), bf16),
            pltpu.VMEM((groups, chunks) + block, bf16),
            pltpu.VMEM((groups, chunks) + block, bf16),
            pltpu.VMEM((groups, chunks) + block, bf16),
            pltpu.VMEM((groups, chips - 1, 2) + block, bf16),
            pltpu.VMEM((chunks, half_rows, HEAD_SIZE), f32),
            pltpu.VMEM((chunks, half_rows, HEAD_SIZE), f32),
            pltpu.VMEM((2, most, lanes), bf16),
            pltpu.VMEM((2, most, lanes), bf16),
            pltpu.VMEM((n * half_rows, rows), f32),
            pltpu.VMEM((most, rows), f32),
            pltpu.VMEM((1, n * rows), jnp.int32),
            pltpu.VMEM((n * rows, HEAD_SIZE), f32),
            pltpu.VMEM((1, rows), jnp.int32),
            pltpu.VMEM((rows, HEAD_SIZE), f32),
            pltpu.VMEM((depth * chips, 1, rows), jnp.int32),
            pltpu.VMEM((1, rows), jnp.int32),
            pltpu.VMEM((1, rows), jnp.int32),
            dma((5,)),
            dma,
            dma((groups, chips - 1)),
            dma,
            dma,
            dma((groups, chips - 1)),
            dma,
            dma((groups, chips - 1)),
            dma,
            dma,
            dma,
            dma((6,)),
        ],
        compiler_params=pltpu.CompilerParams(
            collective_id=0, has_side_effects=True, vmem_limit_bytes=56 * 1024 * 1024
        ),
    )(queries[0], keys[0], values[0], cotangent[0], live, docs)
    shapes = ((rows, q_width),) * 2 + ((rows, kv_width),) * 2
    outputs = pl.pallas_call(
        functools.partial(store_kernel, float(depth * n * rows)),
        out_shape=tuple(jax.ShapeDtypeStruct(shape, bf16) for shape in shapes),
        in_specs=[vmem] * 5,
        out_specs=(anywhere,) * 4,
        scratch_shapes=[pltpu.VMEM(shape, bf16) for shape in shapes[1:]] + [dma((3 + groups,))],
        compiler_params=pltpu.CompilerParams(vmem_limit_bytes=16 * 1024 * 1024),
    )(*results)
    return tuple(output[None] for output in outputs)


def solution(mesh):
    wide = P("dp", "ctx", None)
    return jax.shard_map(
        functools.partial(on_device, mesh.shape["ctx"], mesh.shape["dp"]),
        mesh=mesh,
        in_specs=(wide, wide, wide, wide, P("dp", "ctx"), P("dp", None)),
        out_specs=(wide, wide, wide, wide),
        check_vma=False,
    )
```

```python
import functools
import math

import jax
import jax.numpy as jnp
from jax import lax
from jax.experimental import pallas as pl
from jax.experimental.pallas import tpu as pltpu
from jax.sharding import PartitionSpec as P

HEAD_SIZE = 128
MESH = pl.DeviceIdType.MESH
masked_fill = -1e30
f32, bf16 = jnp.float32, jnp.bfloat16


def matmul(a, b):
    return jnp.dot(a, b, preferred_element_type=f32)


def matmul_nt(a, b):
    return lax.dot_general(a, b, (((1,), (1,)), ((), ())), preferred_element_type=f32)


def on(condition, action):
    if isinstance(condition, bool):
        if condition:
            action()
    else:
        pl.when(condition)(action)


def when(condition):
    return functools.partial(on, condition)


def one(condition):
    return int(condition) if isinstance(condition, bool) else jnp.where(condition, 1, 0)


def rem(a, b):
    return a % b if isinstance(a, int) else lax.rem(a, b)


def negate(condition):
    return not condition if isinstance(condition, bool) else jnp.logical_not(condition)


def device_part(
    me, n, depth, q_hbm, k_hbm, v_hbm, c_hbm, live_hbm, docs_hbm,
    att, gq, kg_ref, vg_ref, total_ref,
    q, cot, kv, tx, px, rx, acc_k, acc_v, held_p, held_s, bias_a, bias_b,
    docs_ref, doc_col, live_row, live_rows, live_all, live_sum, live_pair,
    in_sem, far_sent, far_got, pass_sent, own_got, pass_got,
    part_sent, part_got, part_own, back_sent, back_got, live_sem,
):
    rows = q.shape[0]
    half_rows = rows // 2
    groups = kv.shape[0]
    width = q.shape[1] // groups
    heads = width // HEAD_SIZE
    lanes = heads * half_rows
    chunks = 2 * n
    chips = n // 2
    few = 2
    my_dp = lax.axis_index("dp")
    chip, core = me // 2, rem(me, 2)
    partner = me + 1 - 2 * core
    near = chip == 0
    root = my_dp == 0
    exp_scale = math.log2(math.e) / math.sqrt(HEAD_SIZE)

    def chunk_of(device, half):
        return device if half == 0 else chunks - 1 - device

    def needs(device, chunk):
        first = chunk <= device
        second = (chunk >= n - 1 - device) & (chunk <= chunks - 1 - device)
        return first | second

    def chip_needs(a_chip, chunk):
        return needs(2 * a_chip, chunk) | needs(2 * a_chip + 1, chunk)

    def chip_ahead(k):
        return rem(chip + k, chips)

    def chip_behind(k):
        return rem(chip + chips - k, chips)

    def cross(a_chip):
        return 2 * a_chip + 1 - core

    def level(a_chip):
        return 2 * a_chip + core

    def across(k):
        return cross(chip_ahead(k))

    barrier = pltpu.get_barrier_semaphore()

    def greet(dp, ctx):
        pl.semaphore_signal(barrier, inc=1, device_id=(dp, ctx), device_id_type=MESH)

    greet(my_dp, partner)
    for k in range(1, chips):
        greet(my_dp, across(k))

    def mine(g, half, which):
        source = k_hbm if which == 0 else v_hbm
        columns = pl.ds(pl.multiple_of(g * HEAD_SIZE, HEAD_SIZE), HEAD_SIZE)
        return source.at[pl.ds(half * half_rows, half_rows), columns]

    def own_copy(g, half, which):
        return pltpu.make_async_copy(
            mine(g, half, which), kv.at[g, chunk_of(me, half), which], in_sem.at[0]
        )

    live_copy = pltpu.make_async_copy(live_hbm, live_row, in_sem.at[1])
    docs_copy = pltpu.make_async_copy(docs_hbm, docs_ref, in_sem.at[2])
    q_copy = pltpu.make_async_copy(q_hbm, q, in_sem.at[3])
    c_copy = pltpu.make_async_copy(c_hbm, cot, in_sem.at[4])

    def start_loads():
        for g in range(groups):
            for half in range(2):
                for which in range(2):
                    own_copy(g, half, which).start()
        live_copy.start()
        docs_copy.start()
        c_copy.start()
        q_copy.start()

    on(near, start_loads)

    @when(root)
    def _():
        def greet_dp(d, carry):
            greet(d, me)
            for k in range(1, chips):
                greet(d, across(k))
            return carry

        lax.fori_loop(1, depth, greet_dp, 0)

    def chunk_copy(source, target, sent, got, device):
        return pltpu.make_async_remote_copy(
            src_ref=source, dst_ref=target, send_sem=sent, recv_sem=got,
            device_id=device, device_id_type=MESH,
        )

    def far_copy(g, k, half, which):
        return chunk_copy(
            mine(g, half, which), kv.at[g, chunk_of(me, half), which],
            far_sent, far_got.at[g, k - 1], (my_dp, across(k)),
        )

    def pass_copy(g, k, chunk):
        got = own_got if k == 0 else pass_got.at[g, k - 1]
        return chunk_copy(kv.at[g, chunk], kv.at[g, chunk], pass_sent, got, (my_dp, partner))

    def part_copy(g, k, chunk):
        got = part_own if k == 0 else part_got.at[g, k - 1]
        return chunk_copy(tx.at[g, chunk], px.at[g, chunk], part_sent, got, (my_dp, partner))

    def back_copy(g, k, half, chunk):
        return chunk_copy(
            tx.at[g, chunk], rx.at[g, k - 1, half], back_sent, back_got,
            (my_dp, across(k)),
        )

    def wait_chunks(sem, count, most, whole):
        for c in range(1, most + 1):
            block = kv.at[:, 0:c] if whole else kv.at[0, 0:c]
            on(count == c, lambda: pltpu.make_async_copy(block, block, sem).wait())

    def pair(condition):
        return one(condition(0)) + one(condition(1))

    def over_chips(condition):
        count = 0
        for k in range(1, chips):
            count += pair(lambda half: condition(k, half))
        return count

    def sends_far(k, half):
        return chip_needs(chip_ahead(k), chunk_of(me, half))

    def gets_far(k, half):
        return chip_needs(chip, chunk_of(cross(chip_behind(k)), half))

    def passes(k, half):
        return needs(partner, chunk_of(cross(chip_behind(k)), half))

    def gets_passed(k, half):
        return needs(me, chunk_of(level(chip_behind(k)), half))

    def parts_out(k, half):
        return needs(me, chunk_of(level(chip_ahead(k)), half))

    def gets_part(k, half):
        return needs(partner, chunk_of(cross(chip_ahead(k)), half))

    def sends_back(k, half):
        return chip_needs(chip, chunk_of(cross(chip_ahead(k)), half))

    def gets_back(k, half):
        return chip_needs(chip_behind(k), chunk_of(me, half))

    def shares(half):
        return needs(partner, chunk_of(me, half))

    def shared(half):
        return needs(me, chunk_of(partner, half))

    def arrive(g):
        for k in range(1, chips):
            wait_chunks(far_got.at[g, k - 1], pair(lambda half: gets_far(k, half)), 2, False)
            for half in range(2):
                chunk = chunk_of(cross(chip_behind(k)), half)
                on(passes(k, half), lambda: pass_copy(g, k, chunk).start())

    def settle(g):
        for k in range(1, chips):
            wait_chunks(pass_got.at[g, k - 1], pair(lambda half: gets_passed(k, half)), 2, False)

    def alone(k, half):
        return sends_back(k, half) & negate(gets_part(k, half))

    def send_parts(g):
        for k in range(1, chips):
            for half in range(2):
                chunk = chunk_of(cross(chip_ahead(k)), half)
                on(alone(k, half), lambda: back_copy(g, k, half, chunk).start())
        for k in range(1, chips):
            for half in range(2):
                chunk = chunk_of(level(chip_ahead(k)), half)
                on(parts_out(k, half), lambda: part_copy(g, k, chunk).start())
        for half in range(2):
            chunk = chunk_of(partner, half)
            on(shared(half), lambda: part_copy(g, 0, chunk).start())

    def combine(g):
        for k in range(1, chips):
            wait_chunks(part_got.at[g, k - 1], pair(lambda half: gets_part(k, half)), 2, False)
            for half in range(2):
                chunk = chunk_of(cross(chip_ahead(k)), half)

                @when(gets_part(k, half))
                def _(k=k, half=half, chunk=chunk):
                    tx[g, chunk] = (tx[g, chunk].astype(f32) + px[g, chunk].astype(f32)).astype(
                        bf16
                    )
                    back_copy(g, k, half, chunk).start()

    def live_copy_to(k):
        device = me if k == 0 else across(k)
        return chunk_copy(
            live_hbm, live_all.at[my_dp * chips + k], live_sem.at[0], live_sem.at[1], (0, device)
        )

    def pair_copy():
        return chunk_copy(
            live_sum, live_pair, live_sem.at[2], live_sem.at[3], (my_dp, partner)
        )

    def total_copy(d):
        return chunk_copy(total_ref, total_ref, live_sem.at[4], live_sem.at[5], (d, me))

    def wait_rows(sem, count):
        block = live_all.at[0:count]
        pltpu.make_async_copy(block, block, sem).wait()

    def gather_live():
        wait_rows(live_sem.at[1], depth * chips - 1)
        live_sum[...] = live_row[...] + jnp.sum(live_all[1:], axis=0)
        pair_copy().start()

    def spread_live():
        pair_copy().wait_recv()
        total_ref[...] = live_sum[...] + live_pair[...]

        def spread(d, carry):
            total_copy(d).start()
            return carry

        lax.fori_loop(1, depth, spread, 0)

    own = kv.at[:, 0:2]
    pl.semaphore_wait(barrier, chips + jnp.where(root, 0, chips))
    for k in range(1, chips):
        live_copy_to(k).start()

    def send_keys(g, carry):
        for k in range(1, chips):
            for half in range(2):

                @when(sends_far(k, half))
                def _(k=k, half=half):
                    far_copy(g, k, half, 0).start()
                    far_copy(g, k, half, 1).start()

        return carry

    lax.fori_loop(0, groups, send_keys, 0)
    on(negate(near), start_loads)
    pltpu.make_async_copy(own, own, in_sem.at[0]).wait()

    def share_keys(g, carry):
        for half in range(2):
            chunk = chunk_of(me, half)
            on(shares(half), lambda: pass_copy(g, 0, chunk).start())
        return carry

    lax.fori_loop(0, groups, share_keys, 0)
    on(negate(root), lambda: live_copy_to(0).start())

    def clear(chunk, carry):
        enters = (rem(chunk, 2) != core) & (chunk // 2 != chip)
        held = needs(me, chunk) | (enters & chip_needs(chip, chunk))

        @when(negate(held))
        def _():
            for g in range(groups):
                kv[g, chunk] = jnp.zeros(kv.shape[2:], bf16)

        return carry

    lax.fori_loop(0, n, clear, 0)
    tx[...] = jnp.zeros(tx.shape, bf16)
    acc_k[...] = jnp.zeros(acc_k.shape, f32)
    acc_v[...] = jnp.zeros(acc_v.shape, f32)

    docs_copy.wait()
    for b in range(doc_col.shape[0] // HEAD_SIZE):
        piece = docs_ref[0:1, b * HEAD_SIZE:(b + 1) * HEAD_SIZE].astype(f32)
        doc_col[b * HEAD_SIZE:(b + 1) * HEAD_SIZE, :] = jnp.transpose(
            jnp.broadcast_to(piece, (HEAD_SIZE, HEAD_SIZE))
        )
    first_b = n - 1 - me

    def build(bias, key_chunk, query_chunk):
        size = bias.shape[0]
        start = key_chunk * half_rows
        first_row = start if isinstance(start, int) else pl.multiple_of(start, half_rows)
        key_doc = doc_col[pl.ds(first_row, size), 0:1]
        key_pos = start + lax.broadcasted_iota(jnp.int32, (size, rows), 0)
        query_pos = query_chunk * half_rows + lax.rem(
            lax.broadcasted_iota(jnp.int32, (size, rows), 1), half_rows
        )
        query_doc = jnp.sum(
            jnp.where(key_pos == query_pos, key_doc, 0.0), axis=0, keepdims=True
        )
        allowed = (key_doc == query_doc) & (key_pos <= query_pos)
        bias[...] = jnp.where(allowed, 0.0, masked_fill)

    build(bias_a, 0, chunk_of(me, 0))
    build(bias_b, first_b, chunk_of(me, 1))
    live_copy.wait()
    live_rows[...] = jnp.transpose(
        jnp.broadcast_to(live_row[...].astype(f32), (HEAD_SIZE, rows))
    )
    c_copy.wait()

    def keep_live(j, carry):
        columns = pl.ds(pl.multiple_of(j * HEAD_SIZE, HEAD_SIZE), HEAD_SIZE)
        cot[:, columns] = (cot[:, columns].astype(f32) * live_rows[...]).astype(bf16)
        return carry

    lax.fori_loop(0, groups * heads, keep_live, 0, unroll=4)
    q_copy.wait()
    wait_chunks(own_got, pair(shared), 2, True)

    def stacked(source, g, half):
        return jnp.concatenate(
            [
                source[
                    half * half_rows:(half + 1) * half_rows,
                    pl.ds(pl.multiple_of(g * width + j * HEAD_SIZE, HEAD_SIZE), HEAD_SIZE),
                ]
                for j in range(heads)
            ],
            axis=0,
        )

    def load(unit):
        g, half, start, count = unit
        size = count * half_rows
        window = pl.ds(start, count)
        keys = kv[g, window, 0].reshape(size, HEAD_SIZE)
        values = kv[g, window, 1].reshape(size, HEAD_SIZE)
        return keys, values, stacked(q, g, half), stacked(cot, g, half)

    def products(unit, loaded):
        keys, values, queries, grads = loaded
        bias = (bias_a if unit[1] == 0 else bias_b)[0:keys.shape[0]]
        bias = jnp.concatenate([bias] * (lanes // rows), axis=1)
        return matmul_nt(keys, queries) + bias, matmul_nt(values, grads)

    def soften(scores, pushes):
        peak = jnp.max(scores, axis=0, keepdims=True)
        mass = jnp.exp2((scores - peak) * exp_scale)
        total = jnp.sum(mass, axis=0, keepdims=True)
        weights = mass * (1.0 / total)
        pushed = weights * pushes
        delta = jnp.sum(pushed, axis=0, keepdims=True)
        return weights.astype(bf16), (pushed - weights * delta).astype(bf16)

    def parts(unit, loaded, held, add):
        g, half, start, count = unit
        window = pl.ds(start, count)
        for which, acc in ((1, acc_v), (0, acc_k)):
            part = matmul(held[1 - which], loaded[2 + which])
            part = part.reshape(count, half_rows, HEAD_SIZE)
            if add and half == 0:
                acc[0:count] = part
            elif add:
                part += acc[window]
            tx[g, window, which] = part.astype(bf16)

    def outputs(loaded, held):
        keys, values = loaded[:2]
        return (
            matmul(jnp.transpose(values), held[0]).astype(bf16),
            matmul(jnp.transpose(keys), held[1]).astype(bf16),
        )

    def put(unit, columns):
        g, half = unit[:2]
        low, high = half * half_rows, (half + 1) * half_rows
        for turned, target in zip(columns, (att, gq)):
            result = jnp.transpose(turned)
            for j in range(heads):
                wide = g * width + j * HEAD_SIZE
                if not isinstance(g, int):
                    wide = pl.multiple_of(wide, HEAD_SIZE)
                target[low:high, pl.ds(wide, HEAD_SIZE)] = result[
                    j * half_rows:(j + 1) * half_rows, :
                ]

    def together(units, add):
        loads = [load(unit) for unit in units]
        firsts = [products(unit, loaded) for unit, loaded in zip(units, loads)]
        held = []
        for i, unit in enumerate(units):
            held.append(soften(*firsts[i]))
            if i:
                parts(units[i - 1], loads[i - 1], held[i - 1], add)
        parts(units[-1], loads[-1], held[-1], add)
        for unit, loaded, kept in zip(units, loads, held):
            put(unit, outputs(loaded, kept))

    def late(g):
        return (g, 1, first_b, n + 1)

    def attend(g):
        loaded = load(late(g))
        held = soften(*products(late(g), loaded))
        held_p[...], held_s[...] = held
        parts(late(g), loaded, held, False)

    def finish(g):
        put(late(g), outputs(load(late(g)), (held_p[...], held_s[...])))

    def near_step(g, carry):
        arrive(g)
        on(g > 0, lambda: finish(g - 1))
        on(g > 0, lambda: combine(g - 1))
        settle(g)
        attend(g)
        send_parts(g)
        return carry

    def far_step(g, carry):
        settle(g)
        on(g + 1 < groups, lambda: arrive(g + 1))
        together([(g, 0, 0, n), late(g)], True)
        send_parts(g)
        on(g > 0, lambda: combine(g - 1))
        return carry

    @when(near)
    def _():
        together([(g, 0, 0, few) for g in range(groups)], False)
        lax.fori_loop(0, groups, near_step, 0)

    @when(negate(near))
    def _():
        arrive(0)
        lax.fori_loop(0, groups, far_step, 0)

    on(root, gather_live)
    combine(groups - 1)
    on(root, spread_live)
    on(near, lambda: finish(groups - 1))
    on(negate(root), lambda: total_copy(0).wait_recv())
    wait_chunks(part_own, pair(shares), 2, True)
    wait_chunks(back_got, over_chips(gets_back), chunks - 2, True)

    def reduce_step(g, carry):
        columns = pl.ds(pl.multiple_of(g * HEAD_SIZE, HEAD_SIZE), HEAD_SIZE)
        for half in range(2):
            mine = chunk_of(me, half)
            low, high = half * half_rows, (half + 1) * half_rows
            kg_ref[low:high, columns] = tx[g, mine, 0].astype(f32)
            vg_ref[low:high, columns] = tx[g, mine, 1].astype(f32)

            @when(shares(half))
            def _(mine=mine, low=low, high=high):
                kg_ref[low:high, columns] += px[g, mine, 0].astype(f32)
                vg_ref[low:high, columns] += px[g, mine, 1].astype(f32)

            for k in range(1, chips):

                @when(gets_back(k, half))
                def _(k=k, half=half, low=low, high=high):
                    kg_ref[low:high, columns] += rx[g, k - 1, half, 0].astype(f32)
                    vg_ref[low:high, columns] += rx[g, k - 1, half, 1].astype(f32)

        return carry

    lax.fori_loop(0, groups, reduce_step, 0)

    wait_chunks(far_sent, over_chips(sends_far), chunks - 2, True)
    wait_chunks(pass_sent, over_chips(passes) + pair(shares), chunks, True)
    wait_chunks(part_sent, over_chips(parts_out) + pair(shared), chunks, True)
    wait_chunks(back_sent, over_chips(sends_back), chunks - 2, True)

    @when(root)
    def _():
        wait_rows(live_sem.at[0], chips - 1)
        pair_copy().wait_send()
        wait_rows(live_sem.at[4], depth - 1)

    on(negate(root), lambda: wait_rows(live_sem.at[0], chips))


def kernel(n, *refs):
    me = lax.axis_index("ctx")
    if n > 4:
        device_part(me, n, *refs)
        return
    for device in range(n):
        when(me == device)(functools.partial(device_part, device, n, *refs))


def store_kernel(
    scale, att, gq32, kg32, vg32, total_ref, att_out, gq_out, kg_out, vg_out, gq, kg, vg, sem
):
    copies = []

    def put(source, target):
        copies.append(pltpu.make_async_copy(source, target, sem.at[len(copies)]))
        copies[-1].start()

    put(att, att_out)
    ratio = scale / jnp.sum(total_ref[...].astype(f32), axis=1, keepdims=True)
    slope_ratio = ratio * (1.0 / math.sqrt(HEAD_SIZE))
    pieces = sem.shape[0] - 3
    width = gq.shape[1] // pieces
    for g in range(pieces):
        wide = pl.ds(g * width, width)
        gq[:, wide] = (gq32[:, wide].astype(f32) * slope_ratio).astype(bf16)
        put(gq.at[:, wide], gq_out.at[:, wide])
    kg[...] = (kg32[...] * slope_ratio).astype(bf16)
    put(kg, kg_out)
    vg[...] = (vg32[...] * ratio).astype(bf16)
    put(vg, vg_out)
    for copy in copies:
        copy.wait()


def on_device(n, depth, queries, keys, values, cotangent, live, docs):
    rows, q_width = queries.shape[1:]
    kv_width = keys.shape[2]
    groups = kv_width // HEAD_SIZE
    width = q_width // groups
    half_rows = rows // 2
    lanes = width // HEAD_SIZE * half_rows
    chunks = 2 * n
    chips = n // 2
    if n % 2 or n < 4 or depth < 2:
        raise ValueError("mesh")
    anywhere = pl.BlockSpec(memory_space=pl.ANY)
    vmem = pl.BlockSpec(memory_space=pltpu.VMEM)
    dma = pltpu.SemaphoreType.DMA
    block = (2, half_rows, HEAD_SIZE)
    most = (n + 1) * half_rows
    results = pl.pallas_call(
        functools.partial(kernel, n, depth),
        out_shape=(
            pltpu.VMEM((rows, q_width), bf16),
            pltpu.VMEM((rows, q_width), bf16),
            pltpu.VMEM((rows, kv_width), f32),
            pltpu.VMEM((rows, kv_width), f32),
            pltpu.VMEM((1, rows), jnp.int32),
        ),
        in_specs=[anywhere] * 6,
        out_specs=(vmem,) * 5,
        scratch_shapes=[
            pltpu.VMEM((rows, q_width), bf16),
            pltpu.VMEM((rows, q_width), bf16),
            pltpu.VMEM((groups, chunks) + block, bf16),
            pltpu.VMEM((groups, chunks) + block, bf16),
            pltpu.VMEM((groups, chunks) + block, bf16),
            pltpu.VMEM((groups, chips - 1, 2) + block, bf16),
            pltpu.VMEM((chunks, half_rows, HEAD_SIZE), f32),
            pltpu.VMEM((chunks, half_rows, HEAD_SIZE), f32),
            pltpu.VMEM((most, lanes), bf16),
            pltpu.VMEM((most, lanes), bf16),
            pltpu.VMEM((n * half_rows, rows), f32),
            pltpu.VMEM((most, rows), f32),
            pltpu.VMEM((1, n * rows), jnp.int32),
            pltpu.VMEM((n * rows, HEAD_SIZE), f32),
            pltpu.VMEM((1, rows), jnp.int32),
            pltpu.VMEM((rows, HEAD_SIZE), f32),
            pltpu.VMEM((depth * chips, 1, rows), jnp.int32),
            pltpu.VMEM((1, rows), jnp.int32),
            pltpu.VMEM((1, rows), jnp.int32),
            dma((5,)),
            dma,
            dma((groups, chips - 1)),
            dma,
            dma,
            dma((groups, chips - 1)),
            dma,
            dma((groups, chips - 1)),
            dma,
            dma,
            dma,
            dma((6,)),
        ],
        compiler_params=pltpu.CompilerParams(
            collective_id=0, has_side_effects=True, vmem_limit_bytes=56 * 1024 * 1024
        ),
    )(queries[0], keys[0], values[0], cotangent[0], live, docs)
    shapes = ((rows, q_width),) * 2 + ((rows, kv_width),) * 2
    outputs = pl.pallas_call(
        functools.partial(store_kernel, float(depth * n * rows)),
        out_shape=tuple(jax.ShapeDtypeStruct(shape, bf16) for shape in shapes),
        in_specs=[vmem] * 5,
        out_specs=(anywhere,) * 4,
        scratch_shapes=[pltpu.VMEM(shape, bf16) for shape in shapes[1:]] + [dma((3 + groups,))],
        compiler_params=pltpu.CompilerParams(vmem_limit_bytes=16 * 1024 * 1024),
    )(*results)
    return tuple(output[None] for output in outputs)


def solution(mesh):
    wide = P("dp", "ctx", None)
    return jax.shard_map(
        functools.partial(on_device, mesh.shape["ctx"], mesh.shape["dp"]),
        mesh=mesh,
        in_specs=(wide, wide, wide, wide, P("dp", "ctx"), P("dp", None)),
        out_specs=(wide, wide, wide, wide),
        check_vma=False,
    )
```

```python
import functools
import math

import jax
import jax.numpy as jnp
from jax import lax
from jax.experimental import pallas as pl
from jax.experimental.pallas import tpu as pltpu
from jax.sharding import PartitionSpec as P

HEAD_SIZE = 128
MESH = pl.DeviceIdType.MESH
masked_fill = -1e30
f32, bf16 = jnp.float32, jnp.bfloat16


def matmul(a, b):
    return jnp.dot(a, b, preferred_element_type=f32)


def matmul_nt(a, b):
    return lax.dot_general(a, b, (((1,), (1,)), ((), ())), preferred_element_type=f32)


def on(condition, action):
    if isinstance(condition, bool):
        if condition:
            action()
    else:
        pl.when(condition)(action)


def when(condition):
    return functools.partial(on, condition)


def one(condition):
    return int(condition) if isinstance(condition, bool) else jnp.where(condition, 1, 0)


def rem(a, b):
    return a % b if isinstance(a, int) else lax.rem(a, b)


def negate(condition):
    return not condition if isinstance(condition, bool) else jnp.logical_not(condition)


def device_part(
    me, n, depth, q_hbm, k_hbm, v_hbm, c_hbm, live_hbm, docs_hbm,
    att, gq, kg_ref, vg_ref, total_ref,
    q, cot, kv, tx, px, rx, acc_k, acc_v, held_p, held_s, bias_a, bias_b,
    docs_ref, doc_col, live_row, live_rows, live_all, live_sum, live_pair,
    in_sem, far_sent, far_got, pass_sent, own_got, pass_got,
    part_sent, part_got, part_own, back_sent, back_got, live_sem,
):
    rows = q.shape[0]
    half_rows = rows // 2
    groups = kv.shape[0]
    width = q.shape[1] // groups
    heads = width // HEAD_SIZE
    lanes = heads * half_rows
    chunks = 2 * n
    chips = n // 2
    few = 2
    my_dp = lax.axis_index("dp")
    chip, core = me // 2, rem(me, 2)
    partner = me + 1 - 2 * core
    near = chip == 0
    root = my_dp == 0
    first_count = me + 1 if isinstance(me, int) else None
    exp_scale = math.log2(math.e) / math.sqrt(HEAD_SIZE)

    def chunk_of(device, half):
        return device if half == 0 else chunks - 1 - device

    def needs(device, chunk):
        first = chunk <= device
        second = (chunk >= n - 1 - device) & (chunk <= chunks - 1 - device)
        return first | second

    def chip_needs(a_chip, chunk):
        return needs(2 * a_chip, chunk) | needs(2 * a_chip + 1, chunk)

    def chip_ahead(k):
        return rem(chip + k, chips)

    def chip_behind(k):
        return rem(chip + chips - k, chips)

    def cross(a_chip):
        return 2 * a_chip + 1 - core

    def level(a_chip):
        return 2 * a_chip + core

    def across(k):
        return cross(chip_ahead(k))

    barrier = pltpu.get_barrier_semaphore()

    def greet(dp, ctx):
        pl.semaphore_signal(barrier, inc=1, device_id=(dp, ctx), device_id_type=MESH)

    greet(my_dp, partner)
    for k in range(1, chips):
        greet(my_dp, across(k))

    def mine(g, half, which):
        source = k_hbm if which == 0 else v_hbm
        columns = pl.ds(pl.multiple_of(g * HEAD_SIZE, HEAD_SIZE), HEAD_SIZE)
        return source.at[pl.ds(half * half_rows, half_rows), columns]

    def own_copy(g, half, which):
        return pltpu.make_async_copy(
            mine(g, half, which), kv.at[g, chunk_of(me, half), which], in_sem.at[0]
        )

    live_copy = pltpu.make_async_copy(live_hbm, live_row, in_sem.at[1])
    docs_copy = pltpu.make_async_copy(docs_hbm, docs_ref, in_sem.at[2])
    q_copy = pltpu.make_async_copy(q_hbm, q, in_sem.at[3])
    c_copy = pltpu.make_async_copy(c_hbm, cot, in_sem.at[4])

    def start_loads():
        for g in range(groups):
            for half in range(2):
                for which in range(2):
                    own_copy(g, half, which).start()
        live_copy.start()
        docs_copy.start()
        c_copy.start()
        q_copy.start()

    on(near, start_loads)

    @when(root)
    def _():
        def greet_dp(d, carry):
            greet(d, me)
            for k in range(1, chips):
                greet(d, across(k))
            return carry

        lax.fori_loop(1, depth, greet_dp, 0)

    def chunk_copy(source, target, sent, got, device):
        return pltpu.make_async_remote_copy(
            src_ref=source, dst_ref=target, send_sem=sent, recv_sem=got,
            device_id=device, device_id_type=MESH,
        )

    def far_copy(g, k, half, which):
        return chunk_copy(
            mine(g, half, which), kv.at[g, chunk_of(me, half), which],
            far_sent, far_got.at[g, k - 1], (my_dp, across(k)),
        )

    def pass_copy(g, k, chunk):
        got = own_got if k == 0 else pass_got.at[g, k - 1]
        return chunk_copy(kv.at[g, chunk], kv.at[g, chunk], pass_sent, got, (my_dp, partner))

    def part_copy(g, k, chunk):
        got = part_own if k == 0 else part_got.at[g, k - 1]
        return chunk_copy(tx.at[g, chunk], px.at[g, chunk], part_sent, got, (my_dp, partner))

    def back_copy(g, k, half, chunk):
        return chunk_copy(
            tx.at[g, chunk], rx.at[g, k - 1, half], back_sent, back_got,
            (my_dp, across(k)),
        )

    def wait_chunks(sem, count, most, whole):
        for c in range(1, most + 1):
            block = kv.at[:, 0:c] if whole else kv.at[0, 0:c]
            on(count == c, lambda: pltpu.make_async_copy(block, block, sem).wait())

    def pair(condition):
        return one(condition(0)) + one(condition(1))

    def over_chips(condition):
        count = 0
        for k in range(1, chips):
            count += pair(lambda half: condition(k, half))
        return count

    def sends_far(k, half):
        return chip_needs(chip_ahead(k), chunk_of(me, half))

    def gets_far(k, half):
        return chip_needs(chip, chunk_of(cross(chip_behind(k)), half))

    def passes(k, half):
        return needs(partner, chunk_of(cross(chip_behind(k)), half))

    def gets_passed(k, half):
        return needs(me, chunk_of(level(chip_behind(k)), half))

    def parts_out(k, half):
        return needs(me, chunk_of(level(chip_ahead(k)), half))

    def gets_part(k, half):
        return needs(partner, chunk_of(cross(chip_ahead(k)), half))

    def sends_back(k, half):
        return chip_needs(chip, chunk_of(cross(chip_ahead(k)), half))

    def gets_back(k, half):
        return chip_needs(chip_behind(k), chunk_of(me, half))

    def shares(half):
        return needs(partner, chunk_of(me, half))

    def shared(half):
        return needs(me, chunk_of(partner, half))

    def arrive(g):
        for k in range(1, chips):
            wait_chunks(far_got.at[g, k - 1], pair(lambda half: gets_far(k, half)), 2, False)
            for half in range(2):
                chunk = chunk_of(cross(chip_behind(k)), half)
                on(passes(k, half), lambda: pass_copy(g, k, chunk).start())

    def settle(g):
        for k in range(1, chips):
            wait_chunks(pass_got.at[g, k - 1], pair(lambda half: gets_passed(k, half)), 2, False)

    def alone(k, half):
        return sends_back(k, half) & negate(gets_part(k, half))

    def send_parts(g):
        for k in range(1, chips):
            for half in range(2):
                chunk = chunk_of(cross(chip_ahead(k)), half)
                on(alone(k, half), lambda: back_copy(g, k, half, chunk).start())
        for k in range(1, chips):
            for half in range(2):
                chunk = chunk_of(level(chip_ahead(k)), half)
                on(parts_out(k, half), lambda: part_copy(g, k, chunk).start())
        for half in range(2):
            chunk = chunk_of(partner, half)
            on(shared(half), lambda: part_copy(g, 0, chunk).start())

    def combine(g):
        for k in range(1, chips):
            wait_chunks(part_got.at[g, k - 1], pair(lambda half: gets_part(k, half)), 2, False)
            for half in range(2):
                chunk = chunk_of(cross(chip_ahead(k)), half)

                @when(gets_part(k, half))
                def _(k=k, half=half, chunk=chunk):
                    tx[g, chunk] = (tx[g, chunk].astype(f32) + px[g, chunk].astype(f32)).astype(
                        bf16
                    )
                    back_copy(g, k, half, chunk).start()

    def live_copy_to(k):
        device = me if k == 0 else across(k)
        return chunk_copy(
            live_hbm, live_all.at[my_dp * chips + k], live_sem.at[0], live_sem.at[1], (0, device)
        )

    def pair_copy():
        return chunk_copy(
            live_sum, live_pair, live_sem.at[2], live_sem.at[3], (my_dp, partner)
        )

    def total_copy(d):
        return chunk_copy(total_ref, total_ref, live_sem.at[4], live_sem.at[5], (d, me))

    def wait_rows(sem, count):
        block = live_all.at[0:count]
        pltpu.make_async_copy(block, block, sem).wait()

    def gather_live():
        wait_rows(live_sem.at[1], depth * chips - 1)
        live_sum[...] = live_row[...] + jnp.sum(live_all[1:], axis=0)
        pair_copy().start()

    def spread_live():
        pair_copy().wait_recv()
        total_ref[...] = live_sum[...] + live_pair[...]

        def spread(d, carry):
            total_copy(d).start()
            return carry

        lax.fori_loop(1, depth, spread, 0)

    own = kv.at[:, 0:2]
    pl.semaphore_wait(barrier, chips + jnp.where(root, 0, chips))
    for k in range(1, chips):
        live_copy_to(k).start()

    def send_keys(g, carry):
        for k in range(1, chips):
            for half in range(2):

                @when(sends_far(k, half))
                def _(k=k, half=half):
                    far_copy(g, k, half, 0).start()
                    far_copy(g, k, half, 1).start()

        return carry

    lax.fori_loop(0, groups, send_keys, 0)
    on(negate(near), start_loads)
    pltpu.make_async_copy(own, own, in_sem.at[0]).wait()

    def share_keys(g, carry):
        for half in range(2):
            chunk = chunk_of(me, half)
            on(shares(half), lambda: pass_copy(g, 0, chunk).start())
        return carry

    lax.fori_loop(0, groups, share_keys, 0)
    on(negate(root), lambda: live_copy_to(0).start())

    def clear(chunk, carry):
        enters = (rem(chunk, 2) != core) & (chunk // 2 != chip)
        held = needs(me, chunk) | (enters & chip_needs(chip, chunk))

        @when(negate(held))
        def _():
            for g in range(groups):
                kv[g, chunk] = jnp.zeros(kv.shape[2:], bf16)

        return carry

    lax.fori_loop(0, n, clear, 0)
    tx[...] = jnp.zeros(tx.shape, bf16)
    acc_k[...] = jnp.zeros(acc_k.shape, f32)
    acc_v[...] = jnp.zeros(acc_v.shape, f32)

    docs_copy.wait()
    for b in range(doc_col.shape[0] // HEAD_SIZE):
        piece = docs_ref[0:1, b * HEAD_SIZE:(b + 1) * HEAD_SIZE].astype(f32)
        doc_col[b * HEAD_SIZE:(b + 1) * HEAD_SIZE, :] = jnp.transpose(
            jnp.broadcast_to(piece, (HEAD_SIZE, HEAD_SIZE))
        )
    first_b = n - 1 - me

    def build(bias, key_chunk, query_chunk):
        size = bias.shape[0]
        start = key_chunk * half_rows
        first_row = start if isinstance(start, int) else pl.multiple_of(start, half_rows)
        key_doc = doc_col[pl.ds(first_row, size), 0:1]
        key_pos = start + lax.broadcasted_iota(jnp.int32, (size, rows), 0)
        query_pos = query_chunk * half_rows + lax.rem(
            lax.broadcasted_iota(jnp.int32, (size, rows), 1), half_rows
        )
        query_doc = jnp.sum(
            jnp.where(key_pos == query_pos, key_doc, 0.0), axis=0, keepdims=True
        )
        allowed = (key_doc == query_doc) & (key_pos <= query_pos)
        bias[...] = jnp.where(allowed, 0.0, masked_fill)

    build(bias_a, 0, chunk_of(me, 0))
    build(bias_b, first_b, chunk_of(me, 1))
    live_copy.wait()
    live_rows[...] = jnp.transpose(
        jnp.broadcast_to(live_row[...].astype(f32), (HEAD_SIZE, rows))
    )
    c_copy.wait()

    def keep_live(j, carry):
        columns = pl.ds(pl.multiple_of(j * HEAD_SIZE, HEAD_SIZE), HEAD_SIZE)
        cot[:, columns] = (cot[:, columns].astype(f32) * live_rows[...]).astype(bf16)
        return carry

    lax.fori_loop(0, groups * heads, keep_live, 0, unroll=4)
    q_copy.wait()
    wait_chunks(own_got, pair(shared), 2, True)

    def stacked(source, g, half):
        return jnp.concatenate(
            [
                source[
                    half * half_rows:(half + 1) * half_rows,
                    pl.ds(pl.multiple_of(g * width + j * HEAD_SIZE, HEAD_SIZE), HEAD_SIZE),
                ]
                for j in range(heads)
            ],
            axis=0,
        )

    def load(unit):
        g, half, start, count = unit
        size = count * half_rows
        window = pl.ds(start, count)
        keys = kv[g, window, 0].reshape(size, HEAD_SIZE)
        values = kv[g, window, 1].reshape(size, HEAD_SIZE)
        return keys, values, stacked(q, g, half), stacked(cot, g, half)

    def products(unit, loaded):
        keys, values, queries, grads = loaded
        bias = (bias_a if unit[1] == 0 else bias_b)[0:keys.shape[0]]
        bias = jnp.concatenate([bias] * (lanes // rows), axis=1)
        return matmul_nt(keys, queries) + bias, matmul_nt(values, grads)

    def soften(scores, pushes):
        peak = jnp.max(scores, axis=0, keepdims=True)
        mass = jnp.exp2((scores - peak) * exp_scale)
        total = jnp.sum(mass, axis=0, keepdims=True)
        weights = mass * (1.0 / total)
        pushed = weights * pushes
        delta = jnp.sum(pushed, axis=0, keepdims=True)
        return weights.astype(bf16), (pushed - weights * delta).astype(bf16)

    def parts(unit, loaded, held, add):
        g, half, start, count = unit
        window = pl.ds(start, count)
        for which, acc in ((1, acc_v), (0, acc_k)):
            part = matmul(held[1 - which], loaded[2 + which])
            part = part.reshape(count, half_rows, HEAD_SIZE)
            if add and half == 0:
                acc[0:count] = part
            elif add:
                part += acc[window]
            tx[g, window, which] = part.astype(bf16)

    def outputs(loaded, held):
        keys, values = loaded[:2]
        return (
            matmul(jnp.transpose(values), held[0]).astype(bf16),
            matmul(jnp.transpose(keys), held[1]).astype(bf16),
        )

    def put(unit, columns):
        g, half = unit[:2]
        low, high = half * half_rows, (half + 1) * half_rows
        for turned, target in zip(columns, (att, gq)):
            result = jnp.transpose(turned)
            for j in range(heads):
                wide = g * width + j * HEAD_SIZE
                if not isinstance(g, int):
                    wide = pl.multiple_of(wide, HEAD_SIZE)
                target[low:high, pl.ds(wide, HEAD_SIZE)] = result[
                    j * half_rows:(j + 1) * half_rows, :
                ]

    def together(units, add, between):
        loads = [load(unit) for unit in units]
        firsts = [products(unit, loaded) for unit, loaded in zip(units, loads)]
        held = []
        for i, unit in enumerate(units):
            held.append(soften(*firsts[i]))
            if i:
                parts(units[i - 1], loads[i - 1], held[i - 1], add)
        parts(units[-1], loads[-1], held[-1], add)
        between()
        for unit, loaded, kept in zip(units, loads, held):
            put(unit, outputs(loaded, kept))

    def late(g):
        return (g, 1, first_b, n + 1)

    def attend(g, between):
        loaded = load(late(g))
        held = soften(*products(late(g), loaded))
        held_p[g], held_s[g] = held
        between()
        parts(late(g), loaded, held, False)

    def finish(g):
        put(late(g), outputs(load(late(g)), (held_p[g], held_s[g])))

    def near_steps():
        arrive(0)
        for g in range(groups):
            settle(g)
            attend(g, lambda: arrive(g + 1) if g + 1 < groups else None)
            send_parts(g)
            if g:
                combine(g - 1)
            if 0 < g < groups - 1:
                finish(g - 1)

    def far_step(g, carry):
        settle(g)
        on(g + 1 < groups, lambda: arrive(g + 1))
        together([(g, 0, 0, first_count or n), late(g)], True, lambda: send_parts(g))
        on(g > 0, lambda: combine(g - 1))
        return carry

    @when(near)
    def _():
        own_count = first_count or few
        together([(g, 0, 0, own_count) for g in range(groups)], False, lambda: None)
        near_steps()

    @when(negate(near))
    def _():
        arrive(0)
        lax.fori_loop(0, groups, far_step, 0)

    on(root, gather_live)
    combine(groups - 1)
    on(root, spread_live)

    @when(near)
    def _():
        finish(groups - 2)
        finish(groups - 1)

    on(negate(root), lambda: total_copy(0).wait_recv())
    wait_chunks(part_own, pair(shares), 2, True)
    wait_chunks(back_got, over_chips(gets_back), chunks - 2, True)

    def reduce_step(g, carry):
        columns = pl.ds(pl.multiple_of(g * HEAD_SIZE, HEAD_SIZE), HEAD_SIZE)
        for half in range(2):
            mine = chunk_of(me, half)
            low, high = half * half_rows, (half + 1) * half_rows
            kg_ref[low:high, columns] = tx[g, mine, 0].astype(f32)
            vg_ref[low:high, columns] = tx[g, mine, 1].astype(f32)

            @when(shares(half))
            def _(mine=mine, low=low, high=high):
                kg_ref[low:high, columns] += px[g, mine, 0].astype(f32)
                vg_ref[low:high, columns] += px[g, mine, 1].astype(f32)

            for k in range(1, chips):

                @when(gets_back(k, half))
                def _(k=k, half=half, low=low, high=high):
                    kg_ref[low:high, columns] += rx[g, k - 1, half, 0].astype(f32)
                    vg_ref[low:high, columns] += rx[g, k - 1, half, 1].astype(f32)

        return carry

    lax.fori_loop(0, groups, reduce_step, 0)

    wait_chunks(far_sent, over_chips(sends_far), chunks - 2, True)
    wait_chunks(pass_sent, over_chips(passes) + pair(shares), chunks, True)
    wait_chunks(part_sent, over_chips(parts_out) + pair(shared), chunks, True)
    wait_chunks(back_sent, over_chips(sends_back), chunks - 2, True)

    @when(root)
    def _():
        wait_rows(live_sem.at[0], chips - 1)
        pair_copy().wait_send()
        wait_rows(live_sem.at[4], depth - 1)

    on(negate(root), lambda: wait_rows(live_sem.at[0], chips))


def kernel(n, *refs):
    me = lax.axis_index("ctx")
    if n > 4:
        device_part(me, n, *refs)
        return
    for device in range(n):
        when(me == device)(functools.partial(device_part, device, n, *refs))


def store_kernel(
    scale, att, gq32, kg32, vg32, total_ref, att_out, gq_out, kg_out, vg_out, gq, kg, vg, sem
):
    copies = []

    def put(source, target):
        copies.append(pltpu.make_async_copy(source, target, sem.at[len(copies)]))
        copies[-1].start()

    put(att, att_out)
    ratio = scale / jnp.sum(total_ref[...].astype(f32), axis=1, keepdims=True)
    slope_ratio = ratio * (1.0 / math.sqrt(HEAD_SIZE))
    pieces = sem.shape[0] - 3
    width = gq.shape[1] // pieces
    for g in range(pieces):
        wide = pl.ds(g * width, width)
        gq[:, wide] = (gq32[:, wide].astype(f32) * slope_ratio).astype(bf16)
        put(gq.at[:, wide], gq_out.at[:, wide])
    kg[...] = (kg32[...] * slope_ratio).astype(bf16)
    put(kg, kg_out)
    vg[...] = (vg32[...] * ratio).astype(bf16)
    put(vg, vg_out)
    for copy in copies:
        copy.wait()


def on_device(n, depth, queries, keys, values, cotangent, live, docs):
    rows, q_width = queries.shape[1:]
    kv_width = keys.shape[2]
    groups = kv_width // HEAD_SIZE
    width = q_width // groups
    half_rows = rows // 2
    lanes = width // HEAD_SIZE * half_rows
    chunks = 2 * n
    chips = n // 2
    if n % 2 or n < 4 or depth < 2:
        raise ValueError("mesh")
    anywhere = pl.BlockSpec(memory_space=pl.ANY)
    vmem = pl.BlockSpec(memory_space=pltpu.VMEM)
    dma = pltpu.SemaphoreType.DMA
    block = (2, half_rows, HEAD_SIZE)
    most = (n + 1) * half_rows
    results = pl.pallas_call(
        functools.partial(kernel, n, depth),
        out_shape=(
            pltpu.VMEM((rows, q_width), bf16),
            pltpu.VMEM((rows, q_width), bf16),
            pltpu.VMEM((rows, kv_width), f32),
            pltpu.VMEM((rows, kv_width), f32),
            pltpu.VMEM((1, rows), jnp.int32),
        ),
        in_specs=[anywhere] * 6,
        out_specs=(vmem,) * 5,
        scratch_shapes=[
            pltpu.VMEM((rows, q_width), bf16),
            pltpu.VMEM((rows, q_width), bf16),
            pltpu.VMEM((groups, chunks) + block, bf16),
            pltpu.VMEM((groups, chunks) + block, bf16),
            pltpu.VMEM((groups, chunks) + block, bf16),
            pltpu.VMEM((groups, chips - 1, 2) + block, bf16),
            pltpu.VMEM((chunks, half_rows, HEAD_SIZE), f32),
            pltpu.VMEM((chunks, half_rows, HEAD_SIZE), f32),
            pltpu.VMEM((groups, most, lanes), bf16),
            pltpu.VMEM((groups, most, lanes), bf16),
            pltpu.VMEM((n * half_rows, rows), f32),
            pltpu.VMEM((most, rows), f32),
            pltpu.VMEM((1, n * rows), jnp.int32),
            pltpu.VMEM((n * rows, HEAD_SIZE), f32),
            pltpu.VMEM((1, rows), jnp.int32),
            pltpu.VMEM((rows, HEAD_SIZE), f32),
            pltpu.VMEM((depth * chips, 1, rows), jnp.int32),
            pltpu.VMEM((1, rows), jnp.int32),
            pltpu.VMEM((1, rows), jnp.int32),
            dma((5,)),
            dma,
            dma((groups, chips - 1)),
            dma,
            dma,
            dma((groups, chips - 1)),
            dma,
            dma((groups, chips - 1)),
            dma,
            dma,
            dma,
            dma((6,)),
        ],
        compiler_params=pltpu.CompilerParams(
            collective_id=0, has_side_effects=True, vmem_limit_bytes=56 * 1024 * 1024
        ),
    )(queries[0], keys[0], values[0], cotangent[0], live, docs)
    shapes = ((rows, q_width),) * 2 + ((rows, kv_width),) * 2
    outputs = pl.pallas_call(
        functools.partial(store_kernel, float(depth * n * rows)),
        out_shape=tuple(jax.ShapeDtypeStruct(shape, bf16) for shape in shapes),
        in_specs=[vmem] * 5,
        out_specs=(anywhere,) * 4,
        scratch_shapes=[pltpu.VMEM(shape, bf16) for shape in shapes[1:]] + [dma((3 + groups,))],
        compiler_params=pltpu.CompilerParams(vmem_limit_bytes=16 * 1024 * 1024),
    )(*results)
    return tuple(output[None] for output in outputs)


def solution(mesh):
    wide = P("dp", "ctx", None)
    return jax.shard_map(
        functools.partial(on_device, mesh.shape["ctx"], mesh.shape["dp"]),
        mesh=mesh,
        in_specs=(wide, wide, wide, wide, P("dp", "ctx"), P("dp", None)),
        out_specs=(wide, wide, wide, wide),
        check_vma=False,
    )
```

```python
import functools
import math

import jax
import jax.numpy as jnp
from jax import lax
from jax.experimental import pallas as pl
from jax.experimental.pallas import tpu as pltpu
from jax.sharding import PartitionSpec as P

HEAD_SIZE = 128
MESH = pl.DeviceIdType.MESH
masked_fill = -1e30
f32, bf16 = jnp.float32, jnp.bfloat16


def matmul(a, b):
    return jnp.dot(a, b, preferred_element_type=f32)


def matmul_nt(a, b):
    return lax.dot_general(a, b, (((1,), (1,)), ((), ())), preferred_element_type=f32)


def on(condition, action):
    if isinstance(condition, bool):
        if condition:
            action()
    else:
        pl.when(condition)(action)


def when(condition):
    return functools.partial(on, condition)


def one(condition):
    return int(condition) if isinstance(condition, bool) else jnp.where(condition, 1, 0)


def rem(a, b):
    return a % b if isinstance(a, int) else lax.rem(a, b)


def negate(condition):
    return not condition if isinstance(condition, bool) else jnp.logical_not(condition)


def device_part(
    me, n, depth, q_hbm, k_hbm, v_hbm, c_hbm, live_hbm, docs_hbm,
    att, gq, kg_ref, vg_ref, total_ref,
    q, cot, kv, tx, px, rx, acc_k, acc_v, held_p, held_s, bias_a, bias_b, early_s, early_p,
    docs_ref, doc_col, live_row, live_rows, live_all, live_sum, live_pair,
    in_sem, far_sent, far_got, pass_sent, own_got, pass_got,
    part_sent, part_got, part_own, back_sent, back_got, live_sem,
):
    rows = q.shape[0]
    half_rows = rows // 2
    groups = kv.shape[0]
    width = q.shape[1] // groups
    heads = width // HEAD_SIZE
    lanes = heads * half_rows
    chunks = 2 * n
    chips = n // 2
    few = 2
    my_dp = lax.axis_index("dp")
    chip, core = me // 2, rem(me, 2)
    partner = me + 1 - 2 * core
    near = chip == 0
    root = my_dp == 0
    split = isinstance(me, int) and not near and n == 2 * few
    first_count = me + 1 if isinstance(me, int) else None
    exp_scale = math.log2(math.e) / math.sqrt(HEAD_SIZE)

    def chunk_of(device, half):
        return device if half == 0 else chunks - 1 - device

    def needs(device, chunk):
        first = chunk <= device
        second = (chunk >= n - 1 - device) & (chunk <= chunks - 1 - device)
        return first | second

    def chip_needs(a_chip, chunk):
        return needs(2 * a_chip, chunk) | needs(2 * a_chip + 1, chunk)

    def chip_ahead(k):
        return rem(chip + k, chips)

    def chip_behind(k):
        return rem(chip + chips - k, chips)

    def cross(a_chip):
        return 2 * a_chip + 1 - core

    def level(a_chip):
        return 2 * a_chip + core

    def across(k):
        return cross(chip_ahead(k))

    barrier = pltpu.get_barrier_semaphore()

    def greet(dp, ctx):
        pl.semaphore_signal(barrier, inc=1, device_id=(dp, ctx), device_id_type=MESH)

    greet(my_dp, partner)
    for k in range(1, chips):
        greet(my_dp, across(k))

    def mine(g, half, which):
        source = k_hbm if which == 0 else v_hbm
        columns = pl.ds(pl.multiple_of(g * HEAD_SIZE, HEAD_SIZE), HEAD_SIZE)
        return source.at[pl.ds(half * half_rows, half_rows), columns]

    def own_copy(g, half, which):
        return pltpu.make_async_copy(
            mine(g, half, which), kv.at[g, chunk_of(me, half), which], in_sem.at[0]
        )

    live_copy = pltpu.make_async_copy(live_hbm, live_row, in_sem.at[1])
    docs_copy = pltpu.make_async_copy(docs_hbm, docs_ref, in_sem.at[2])
    q_copy = pltpu.make_async_copy(q_hbm, q, in_sem.at[3])
    c_copy = pltpu.make_async_copy(c_hbm, cot, in_sem.at[4])

    def start_loads():
        for g in range(groups):
            for half in range(2):
                for which in range(2):
                    own_copy(g, half, which).start()
        live_copy.start()
        docs_copy.start()
        c_copy.start()
        q_copy.start()

    on(near, start_loads)

    @when(root)
    def _():
        def greet_dp(d, carry):
            greet(d, me)
            for k in range(1, chips):
                greet(d, across(k))
            return carry

        lax.fori_loop(1, depth, greet_dp, 0)

    def chunk_copy(source, target, sent, got, device):
        return pltpu.make_async_remote_copy(
            src_ref=source, dst_ref=target, send_sem=sent, recv_sem=got,
            device_id=device, device_id_type=MESH,
        )

    def far_copy(g, k, half, which):
        return chunk_copy(
            mine(g, half, which), kv.at[g, chunk_of(me, half), which],
            far_sent, far_got.at[g, k - 1], (my_dp, across(k)),
        )

    def pass_copy(g, k, chunk):
        got = own_got if k == 0 else pass_got.at[g, k - 1]
        return chunk_copy(kv.at[g, chunk], kv.at[g, chunk], pass_sent, got, (my_dp, partner))

    def part_copy(g, k, chunk, which=None):
        at = (g, chunk) if which is None else (g, chunk, which)
        got = part_own if k == 0 else part_got.at[g, k - 1, which or 0]
        return chunk_copy(tx.at[at], px.at[at], part_sent, got, (my_dp, partner))

    def back_copy(g, k, half, chunk, which=None):
        end = () if which is None else (which,)
        return chunk_copy(
            tx.at[(g, chunk) + end], rx.at[(g, k - 1, half) + end], back_sent, back_got,
            (my_dp, across(k)),
        )

    def wait_chunks(sem, count, most, whole, which=None):
        for c in range(1, most + 1):
            block = kv.at[:, 0:c] if whole else kv.at[0, 0:c]
            if which is not None:
                block = kv.at[0, 0:c, which]
            on(count == c, lambda: pltpu.make_async_copy(block, block, sem).wait())

    def pair(condition):
        return one(condition(0)) + one(condition(1))

    def over_chips(condition):
        count = 0
        for k in range(1, chips):
            count += pair(lambda half: condition(k, half))
        return count

    def sends_far(k, half):
        return chip_needs(chip_ahead(k), chunk_of(me, half))

    def gets_far(k, half):
        return chip_needs(chip, chunk_of(cross(chip_behind(k)), half))

    def passes(k, half):
        return needs(partner, chunk_of(cross(chip_behind(k)), half))

    def gets_passed(k, half):
        return needs(me, chunk_of(level(chip_behind(k)), half))

    def parts_out(k, half):
        return needs(me, chunk_of(level(chip_ahead(k)), half))

    def gets_part(k, half):
        return needs(partner, chunk_of(cross(chip_ahead(k)), half))

    def sends_back(k, half):
        return chip_needs(chip, chunk_of(cross(chip_ahead(k)), half))

    def gets_back(k, half):
        return chip_needs(chip_behind(k), chunk_of(me, half))

    def shares(half):
        return needs(partner, chunk_of(me, half))

    def shared(half):
        return needs(me, chunk_of(partner, half))

    def arrive(g):
        for k in range(1, chips):
            wait_chunks(far_got.at[g, k - 1], pair(lambda half: gets_far(k, half)), 2, False)
            for half in range(2):
                chunk = chunk_of(cross(chip_behind(k)), half)
                on(passes(k, half), lambda: pass_copy(g, k, chunk).start())

    def settle(g):
        for k in range(1, chips):
            wait_chunks(pass_got.at[g, k - 1], pair(lambda half: gets_passed(k, half)), 2, False)

    def alone(k, half):
        return sends_back(k, half) & negate(gets_part(k, half))

    def send_parts(g, which=None):
        for k in range(1, chips):
            for half in range(2):
                chunk = chunk_of(level(chip_ahead(k)), half)
                on(parts_out(k, half), lambda: part_copy(g, k, chunk, which).start())
        for k in range(1, chips):
            for half in range(2):
                chunk = chunk_of(cross(chip_ahead(k)), half)
                on(alone(k, half), lambda: back_copy(g, k, half, chunk, which).start())
        for half in range(2):
            chunk = chunk_of(partner, half)
            on(shared(half), lambda: part_copy(g, 0, chunk, which).start())

    def combine(g, which=None):
        for k in range(1, chips):
            wait_chunks(
                part_got.at[g, k - 1, which or 0], pair(lambda half: gets_part(k, half)), 2,
                False, which,
            )
            for half in range(2):
                chunk = chunk_of(cross(chip_ahead(k)), half)

                @when(gets_part(k, half))
                def _(k=k, half=half, chunk=chunk):
                    at = (g, chunk) if which is None else (g, chunk, which)
                    tx[at] = (tx[at].astype(f32) + px[at].astype(f32)).astype(bf16)
                    back_copy(g, k, half, chunk, which).start()

    def live_copy_to(k):
        device = me if k == 0 else across(k)
        return chunk_copy(
            live_hbm, live_all.at[my_dp * chips + k], live_sem.at[0], live_sem.at[1], (0, device)
        )

    def pair_copy():
        return chunk_copy(
            live_sum, live_pair, live_sem.at[2], live_sem.at[3], (my_dp, partner)
        )

    def total_copy(d):
        return chunk_copy(total_ref, total_ref, live_sem.at[4], live_sem.at[5], (d, me))

    def wait_rows(sem, count):
        block = live_all.at[0:count]
        pltpu.make_async_copy(block, block, sem).wait()

    def gather_live():
        wait_rows(live_sem.at[1], depth * chips - 1)
        live_sum[...] = live_row[...] + jnp.sum(live_all[1:], axis=0)
        pair_copy().start()

    def spread_live():
        pair_copy().wait_recv()
        total_ref[...] = live_sum[...] + live_pair[...]

        def spread(d, carry):
            total_copy(d).start()
            return carry

        lax.fori_loop(1, depth, spread, 0)

    own = kv.at[:, 0:2]
    pl.semaphore_wait(barrier, chips + jnp.where(root, 0, chips))
    for k in range(1, chips):
        live_copy_to(k).start()

    def send_keys(g, carry):
        for k in range(1, chips):
            for half in range(2):

                @when(sends_far(k, half))
                def _(k=k, half=half):
                    far_copy(g, k, half, 0).start()
                    far_copy(g, k, half, 1).start()

        return carry

    lax.fori_loop(0, groups, send_keys, 0)
    on(negate(near), start_loads)
    pltpu.make_async_copy(own, own, in_sem.at[0]).wait()

    def share_keys(g, carry):
        for half in range(2):
            chunk = chunk_of(me, half)
            on(shares(half), lambda: pass_copy(g, 0, chunk).start())
        return carry

    lax.fori_loop(0, groups, share_keys, 0)
    on(negate(root), lambda: live_copy_to(0).start())

    def clear(chunk, carry):
        enters = (rem(chunk, 2) != core) & (chunk // 2 != chip)
        held = needs(me, chunk) | (enters & chip_needs(chip, chunk))

        @when(negate(held))
        def _():
            for g in range(groups):
                kv[g, chunk] = jnp.zeros(kv.shape[2:], bf16)

        return carry

    lax.fori_loop(0, n, clear, 0)
    tx[...] = jnp.zeros(tx.shape, bf16)
    acc_k[...] = jnp.zeros(acc_k.shape, f32)
    acc_v[...] = jnp.zeros(acc_v.shape, f32)

    docs_copy.wait()
    for b in range(doc_col.shape[0] // HEAD_SIZE):
        piece = docs_ref[0:1, b * HEAD_SIZE:(b + 1) * HEAD_SIZE].astype(f32)
        doc_col[b * HEAD_SIZE:(b + 1) * HEAD_SIZE, :] = jnp.transpose(
            jnp.broadcast_to(piece, (HEAD_SIZE, HEAD_SIZE))
        )
    first_b = n - 1 - me

    def build(bias, key_chunk, query_chunk):
        size = bias.shape[0]
        start = key_chunk * half_rows
        first_row = start if isinstance(start, int) else pl.multiple_of(start, half_rows)
        key_doc = doc_col[pl.ds(first_row, size), 0:1]
        key_pos = start + lax.broadcasted_iota(jnp.int32, (size, rows), 0)
        query_pos = query_chunk * half_rows + lax.rem(
            lax.broadcasted_iota(jnp.int32, (size, rows), 1), half_rows
        )
        query_doc = jnp.sum(
            jnp.where(key_pos == query_pos, key_doc, 0.0), axis=0, keepdims=True
        )
        allowed = (key_doc == query_doc) & (key_pos <= query_pos)
        bias[...] = jnp.where(allowed, 0.0, masked_fill)

    build(bias_a, 0, chunk_of(me, 0))
    build(bias_b, first_b, chunk_of(me, 1))
    live_copy.wait()
    live_rows[...] = jnp.transpose(
        jnp.broadcast_to(live_row[...].astype(f32), (HEAD_SIZE, rows))
    )
    c_copy.wait()

    def keep_live(j, carry):
        columns = pl.ds(pl.multiple_of(j * HEAD_SIZE, HEAD_SIZE), HEAD_SIZE)
        cot[:, columns] = (cot[:, columns].astype(f32) * live_rows[...]).astype(bf16)
        return carry

    lax.fori_loop(0, groups * heads, keep_live, 0, unroll=4)
    q_copy.wait()
    wait_chunks(own_got, pair(shared), 2, True)

    def stacked(source, g, half):
        return jnp.concatenate(
            [
                source[
                    half * half_rows:(half + 1) * half_rows,
                    pl.ds(pl.multiple_of(g * width + j * HEAD_SIZE, HEAD_SIZE), HEAD_SIZE),
                ]
                for j in range(heads)
            ],
            axis=0,
        )

    def load(unit):
        g, half, start, count = unit
        size = count * half_rows
        window = pl.ds(start, count)
        keys = kv[g, window, 0].reshape(size, HEAD_SIZE)
        values = kv[g, window, 1].reshape(size, HEAD_SIZE)
        return keys, values, stacked(q, g, half), stacked(cot, g, half)

    def products(unit, loaded):
        keys, values, queries, grads = loaded
        g, half, start, count = unit
        bias = (bias_a if half == 0 else bias_b)[0:keys.shape[0]]
        bias = jnp.concatenate([bias] * (lanes // rows), axis=1)
        if not split:
            return matmul_nt(keys, queries) + bias, matmul_nt(values, grads)
        lead = (few - start) * half_rows
        rest = count * half_rows - lead
        scores = jnp.concatenate(
            [matmul_nt(keys[:lead], queries), early_s[g, half, 0:rest]], axis=0
        )
        pushes = jnp.concatenate(
            [matmul_nt(values[:lead], grads), early_p[g, half, 0:rest]], axis=0
        )
        return scores + bias, pushes

    def prepare(g):
        for unit in ((g, 0, 0, first_count or n), late(g)):
            half, start, count = unit[1:]
            own_chunks = start + count - few
            rest = own_chunks * half_rows
            keys, values, queries, grads = load((g, half, few, own_chunks))
            early_s[g, half, 0:rest] = matmul_nt(keys, queries)
            early_p[g, half, 0:rest] = matmul_nt(values, grads)

    def weigh(scores):
        peak = jnp.max(scores, axis=0, keepdims=True)
        mass = jnp.exp2((scores - peak) * exp_scale)
        return mass * (1.0 / jnp.sum(mass, axis=0, keepdims=True))

    def incline(weights, pushes):
        pushed = weights * pushes
        delta = jnp.sum(pushed, axis=0, keepdims=True)
        return (pushed - weights * delta).astype(bf16)

    def soften(scores, pushes):
        weights = weigh(scores)
        return weights.astype(bf16), incline(weights, pushes)

    def part(unit, loaded, which, held, add):
        g, half, start, count = unit
        window = pl.ds(start, count)
        acc = acc_v if which else acc_k
        result = matmul(held, loaded[2 + which]).reshape(count, half_rows, HEAD_SIZE)
        if add and half == 0:
            acc[0:count] = result
        elif add:
            result += acc[window]
        tx[g, window, which] = result.astype(bf16)

    def parts(unit, loaded, held, add):
        part(unit, loaded, 1, held[0], add)
        part(unit, loaded, 0, held[1], add)

    def outputs(loaded, held):
        keys, values = loaded[:2]
        return (
            matmul(jnp.transpose(values), held[0]).astype(bf16),
            matmul(jnp.transpose(keys), held[1]).astype(bf16),
        )

    def put(unit, columns):
        g, half = unit[:2]
        low, high = half * half_rows, (half + 1) * half_rows
        for turned, target in zip(columns, (att, gq)):
            result = jnp.transpose(turned)
            for j in range(heads):
                wide = g * width + j * HEAD_SIZE
                if not isinstance(g, int):
                    wide = pl.multiple_of(wide, HEAD_SIZE)
                target[low:high, pl.ds(wide, HEAD_SIZE)] = result[
                    j * half_rows:(j + 1) * half_rows, :
                ]

    def together(units, add, between):
        loads = [load(unit) for unit in units]
        firsts = [products(unit, loaded) for unit, loaded in zip(units, loads)]
        held = []
        for i, unit in enumerate(units):
            held.append(soften(*firsts[i]))
            if i:
                parts(units[i - 1], loads[i - 1], held[i - 1], add)
        parts(units[-1], loads[-1], held[-1], add)
        between()
        for unit, loaded, kept in zip(units, loads, held):
            put(unit, outputs(loaded, kept))

    def at_last(units, add):
        g = units[0][0]
        loads = [load(unit) for unit in units]
        firsts = [products(unit, loaded) for unit, loaded in zip(units, loads)]
        weights = [weigh(scores) for scores, _ in firsts]
        rounded = [held.astype(bf16) for held in weights]
        for unit, loaded, held in zip(units, loads, rounded):
            part(unit, loaded, 1, held, add)
        send_parts(g, 1)
        slopes = [incline(held, pushes) for held, (_, pushes) in zip(weights, firsts)]
        for unit, loaded, held in zip(units, loads, slopes):
            part(unit, loaded, 0, held, add)
        send_parts(g, 0)
        return loads, rounded, slopes

    def late(g):
        return (g, 1, first_b, n + 1)

    def attend(g, between):
        loaded = load(late(g))
        held = soften(*products(late(g), loaded))
        held_p[g], held_s[g] = held
        between()
        parts(late(g), loaded, held, False)

    def finish(g):
        put(late(g), outputs(load(late(g)), (held_p[g], held_s[g])))

    def near_steps():
        arrive(0)
        for g in range(groups):
            if g + 2 == groups:
                arrive(g + 1)
            settle(g)
            if g + 1 < groups:
                attend(g, lambda: arrive(g + 1) if g + 2 < groups else None)
                send_parts(g)
            else:
                _, rounded, slopes = at_last([late(g)], False)
                held_p[g], held_s[g] = rounded[0], slopes[0]
            if g:
                combine(g - 1)
            if 0 < g < groups - 1:
                finish(g - 1)

    def far_step(g, carry):
        settle(g)
        arrive(g + 1)
        together([(g, 0, 0, first_count or n), late(g)], True, lambda: send_parts(g))
        on(g > 0, lambda: combine(g - 1))
        return carry

    @when(near)
    def _():
        own_count = first_count or few
        together([(g, 0, 0, own_count) for g in range(groups)], False, lambda: None)
        near_steps()

    @when(negate(near))
    def _():
        for g in range(groups):
            if g == groups // 2:
                arrive(0)
            if split:
                prepare(g)
        lax.fori_loop(0, groups - 1, far_step, 0)
        g = groups - 1
        settle(g)
        units = [(g, 0, 0, first_count or n), late(g)]
        loads, *held = at_last(units, True)
        combine(g - 1)
        for unit, loaded, kept in zip(units, loads, zip(*held)):
            put(unit, outputs(loaded, kept))

    on(root, gather_live)
    combine(groups - 1, 1)
    combine(groups - 1, 0)
    on(root, spread_live)

    @when(near)
    def _():
        finish(groups - 2)
        finish(groups - 1)

    on(negate(root), lambda: total_copy(0).wait_recv())
    wait_chunks(part_own, pair(shares), 2, True)

    def reduce_step(stage, g, carry):
        columns = pl.ds(pl.multiple_of(g * HEAD_SIZE, HEAD_SIZE), HEAD_SIZE)
        for half in range(2):
            mine = chunk_of(me, half)
            low, high = half * half_rows, (half + 1) * half_rows

            def add(target, at, columns=columns, low=low, high=high):
                kg_ref[low:high, columns] += target[at + (0,)].astype(f32)
                vg_ref[low:high, columns] += target[at + (1,)].astype(f32)

            if stage == 0:
                kg_ref[low:high, columns] = tx[g, mine, 0].astype(f32)
                vg_ref[low:high, columns] = tx[g, mine, 1].astype(f32)
                on(shares(half), lambda: add(px, (g, mine)))
                continue
            for k in range(1, chips):
                on(gets_back(k, half), lambda: add(rx, (g, k - 1, half)))

        return carry

    lax.fori_loop(0, groups, functools.partial(reduce_step, 0), 0)
    wait_chunks(back_got, over_chips(gets_back), chunks - 2, True)
    lax.fori_loop(0, groups, functools.partial(reduce_step, 1), 0)

    wait_chunks(far_sent, over_chips(sends_far), chunks - 2, True)
    wait_chunks(pass_sent, over_chips(passes) + pair(shares), chunks, True)
    wait_chunks(part_sent, over_chips(parts_out) + pair(shared), chunks, True)
    wait_chunks(back_sent, over_chips(sends_back), chunks - 2, True)

    @when(root)
    def _():
        wait_rows(live_sem.at[0], chips - 1)
        pair_copy().wait_send()
        wait_rows(live_sem.at[4], depth - 1)

    on(negate(root), lambda: wait_rows(live_sem.at[0], chips))


def kernel(n, *refs):
    me = lax.axis_index("ctx")
    if n > 4:
        device_part(me, n, *refs)
        return
    for device in range(n):
        when(me == device)(functools.partial(device_part, device, n, *refs))


def store_kernel(
    scale, att, gq32, kg32, vg32, total_ref, att_out, gq_out, kg_out, vg_out, gq, kg, vg, sem
):
    copies = []

    def put(source, target):
        copies.append(pltpu.make_async_copy(source, target, sem.at[len(copies)]))
        copies[-1].start()

    put(att, att_out)
    ratio = scale / jnp.sum(total_ref[...].astype(f32), axis=1, keepdims=True)
    slope_ratio = ratio * (1.0 / math.sqrt(HEAD_SIZE))
    pieces = sem.shape[0] - 3
    width = gq.shape[1] // pieces
    for g in range(pieces):
        wide = pl.ds(g * width, width)
        gq[:, wide] = (gq32[:, wide].astype(f32) * slope_ratio).astype(bf16)
        put(gq.at[:, wide], gq_out.at[:, wide])
    kg[...] = (kg32[...] * slope_ratio).astype(bf16)
    put(kg, kg_out)
    vg[...] = (vg32[...] * ratio).astype(bf16)
    put(vg, vg_out)
    for copy in copies:
        copy.wait()


def on_device(n, depth, queries, keys, values, cotangent, live, docs):
    rows, q_width = queries.shape[1:]
    kv_width = keys.shape[2]
    groups = kv_width // HEAD_SIZE
    width = q_width // groups
    half_rows = rows // 2
    lanes = width // HEAD_SIZE * half_rows
    chunks = 2 * n
    chips = n // 2
    if n % 2 or n < 4 or depth < 2:
        raise ValueError("mesh")
    anywhere = pl.BlockSpec(memory_space=pl.ANY)
    vmem = pl.BlockSpec(memory_space=pltpu.VMEM)
    dma = pltpu.SemaphoreType.DMA
    block = (2, half_rows, HEAD_SIZE)
    most = (n + 1) * half_rows
    early = (groups, 2, n * half_rows if n <= 4 else 8, lanes)
    results = pl.pallas_call(
        functools.partial(kernel, n, depth),
        out_shape=(
            pltpu.VMEM((rows, q_width), bf16),
            pltpu.VMEM((rows, q_width), bf16),
            pltpu.VMEM((rows, kv_width), f32),
            pltpu.VMEM((rows, kv_width), f32),
            pltpu.VMEM((1, rows), jnp.int32),
        ),
        in_specs=[anywhere] * 6,
        out_specs=(vmem,) * 5,
        scratch_shapes=[
            pltpu.VMEM((rows, q_width), bf16),
            pltpu.VMEM((rows, q_width), bf16),
            pltpu.VMEM((groups, chunks) + block, bf16),
            pltpu.VMEM((groups, chunks) + block, bf16),
            pltpu.VMEM((groups, chunks) + block, bf16),
            pltpu.VMEM((groups, chips - 1, 2) + block, bf16),
            pltpu.VMEM((chunks, half_rows, HEAD_SIZE), f32),
            pltpu.VMEM((chunks, half_rows, HEAD_SIZE), f32),
            pltpu.VMEM((groups, most, lanes), bf16),
            pltpu.VMEM((groups, most, lanes), bf16),
            pltpu.VMEM((n * half_rows, rows), f32),
            pltpu.VMEM((most, rows), f32),
            pltpu.VMEM(early, f32),
            pltpu.VMEM(early, f32),
            pltpu.VMEM((1, n * rows), jnp.int32),
            pltpu.VMEM((n * rows, HEAD_SIZE), f32),
            pltpu.VMEM((1, rows), jnp.int32),
            pltpu.VMEM((rows, HEAD_SIZE), f32),
            pltpu.VMEM((depth * chips, 1, rows), jnp.int32),
            pltpu.VMEM((1, rows), jnp.int32),
            pltpu.VMEM((1, rows), jnp.int32),
            dma((5,)),
            dma,
            dma((groups, chips - 1)),
            dma,
            dma,
            dma((groups, chips - 1)),
            dma,
            dma((groups, chips - 1, 2)),
            dma,
            dma,
            dma,
            dma((6,)),
        ],
        compiler_params=pltpu.CompilerParams(
            collective_id=0, has_side_effects=True, vmem_limit_bytes=56 * 1024 * 1024
        ),
    )(queries[0], keys[0], values[0], cotangent[0], live, docs)
    shapes = ((rows, q_width),) * 2 + ((rows, kv_width),) * 2
    outputs = pl.pallas_call(
        functools.partial(store_kernel, float(depth * n * rows)),
        out_shape=tuple(jax.ShapeDtypeStruct(shape, bf16) for shape in shapes),
        in_specs=[vmem] * 5,
        out_specs=(anywhere,) * 4,
        scratch_shapes=[pltpu.VMEM(shape, bf16) for shape in shapes[1:]] + [dma((3 + groups,))],
        compiler_params=pltpu.CompilerParams(vmem_limit_bytes=16 * 1024 * 1024),
    )(*results)
    return tuple(output[None] for output in outputs)


def solution(mesh):
    wide = P("dp", "ctx", None)
    return jax.shard_map(
        functools.partial(on_device, mesh.shape["ctx"], mesh.shape["dp"]),
        mesh=mesh,
        in_specs=(wide, wide, wide, wide, P("dp", "ctx"), P("dp", None)),
        out_specs=(wide, wide, wide, wide),
        check_vma=False,
    )
```
